256 devices in a mesh: seq: 32 (over x, z_hi, core), tp: 8 (over z_lo, y).
Axes of the slice: x: 4, y: 4, z: 8 (z_hi: 4, z_lo: 2; z = z_hi * 2 + z_lo), core: 2. Of those that a mesh axis runs over, the one named last changes fastest.
Arguments:
- tokens: bfloat16 [1024, 8192], P('tp', 'seq'), may hold values from -6 to 6
- gate_weight: bfloat16 [8192, 14336], P('seq', 'tp'), may hold values from -0.0625 to 0.0625
- up_weight: bfloat16 [8192, 14336], P('seq', 'tp'), may hold values from -0.0625 to 0.0625
- down_weight: bfloat16 [14336, 8192], P('tp', 'seq'), may hold values from -0.09375 to 0.09375
- masks: int32 [8, 112], P(None, 'tp'), may hold values from 0 to 1, as said below
- cotangent: bfloat16 [1024, 8192], P('tp', 'seq'), may hold values from -6 to 6
Outputs:
- output: bfloat16 [1024, 8192], P('tp', 'seq')
- grad_tokens: bfloat16 [1024, 8192], P('tp', 'seq')
- grad_gate: float32 [8192, 14336], P('seq', 'tp')
- grad_up: float32 [8192, 14336], P('seq', 'tp')
- grad_down: float32 [14336, 8192], P('tp', 'seq')
The draws below stay inside these ranges and needn't reach their ends.
Inputs may be any that keep to these rules, and one draw needn't show every extreme that they name: Each row of masks holds exactly 28 ones. Cut a row into 8 groups of 14 consecutive blocks: in every row one group holds exactly 7 ones, and the remaining ones are spread over the other groups as evenly as possible, so that their counts differ by at most one.
All inputs are finite; a program needn't handle non-finite values.
Results may differ from the reference program's by a relative error of at most 0.0049.
Values may be sent and summed in bfloat16 or wider, within the bound.
No kernel may reach another device: no remote copies, remote signals or barrier semaphores. Data moves between devices by JAX's collectives and lax.ppermute only.
A program may use at most 128 MiB of HBM per device.

```python
import math
import jax
import jax.numpy as jnp

D = 8192
FF = 14336
BLK = 128
ROWBLK = 128
SEQUENCE_TOKENS = 1024
KEEP = 28
N_TP = 8


def draw_masks(key, part):
    block_total = FF // BLK
    kept_total = block_total // 4
    row_blocks = SEQUENCE_TOKENS // ROWBLK
    per_shard = block_total // N_TP
    capacity = 2 * kept_total // N_TP
    remainder = kept_total - capacity
    base_count = remainder // (N_TP - 1)
    extra_count = remainder % (N_TP - 1)

    def one_row(row_key):
        perm_key, selection_key = jax.random.split(row_key)
        order = jax.random.permutation(perm_key, N_TP)
        position = jnp.argsort(order, stable=True).astype(jnp.int32)
        shard_count = jnp.where(position == 0, capacity, base_count + (position - 1 < extra_count).astype(jnp.int32))
        block_rank = jax.vmap(lambda inner_key: jax.random.permutation(inner_key, per_shard))(jax.random.split(selection_key, N_TP))
        chosen = (block_rank < shard_count[:, None]).astype(jnp.int32)
        return chosen.reshape(block_total)
    return jax.vmap(one_row)(jax.random.split(key, row_blocks)).astype(jnp.int32)


def level_of(rng, extent, cuts, least, top_value):
    def one(axis_at, blocks):
        draws = jax.random.uniform(jax.random.fold_in(jax.random.fold_in(rng, 6), axis_at), (blocks,), jnp.float32, least / len(cuts), top_value / len(cuts))
        return jnp.repeat(jnp.exp(draws), extent[axis_at] // blocks).reshape((-1,) + (1,) * (len(extent) - axis_at - 1))

    loudness = one(*cuts[0])
    for cut in cuts[1:]:
        loudness = loudness * one(*cut)
    return loudness


def normal_values(own_key, shape, scale, limit, cuts=(), held_as=jnp.bfloat16):
    drawn = jax.random.normal(own_key, shape, jnp.float32) * scale
    if len(cuts) > 0:
        drawn = level_of(own_key, shape, cuts, -0.22, 0.18) * drawn
    return jnp.clip(drawn, min=-limit, max=limit).astype(held_as)


def setup_inputs(seed: int = 0) -> dict:
    key_of = jax.random.split(jax.random.key(seed), 7)
    tokens = normal_values(key_of[0], (SEQUENCE_TOKENS, D), 1.0, 6.0, ((0, 8), (1, 32)))
    gate_weight = normal_values(key_of[1], (D, FF), D ** -0.5, 0.0625, ((0, 32), (1, 8)))
    up_weight = normal_values(key_of[2], (D, FF), D ** -0.5, 0.0625, ((0, 32), (1, 8)))
    down_weight = normal_values(key_of[3], (FF, D), (KEEP * BLK) ** -0.5, 0.09375, ((0, 8), (1, 32)))
    masks = draw_masks(jax.random.fold_in(key_of[6], 71), 0)
    cotangent = normal_values(key_of[5], (SEQUENCE_TOKENS, D), 1.0, 6.0, ((0, 8), (1, 32)))
    return {"tokens": tokens, "gate_weight": gate_weight, "up_weight": up_weight, "down_weight": down_weight, "masks": masks, "cotangent": cotangent}


def reference(tokens, gate_weight, up_weight, down_weight, masks, cotangent):
    keep = jnp.repeat(jnp.repeat(masks, ROWBLK, axis=0), BLK, axis=1).astype(jnp.float32)
    gate = jnp.dot(tokens, gate_weight, preferred_element_type=jnp.float32)
    up = jnp.dot(tokens, up_weight, preferred_element_type=jnp.float32)
    hidden = (jax.nn.silu(gate) * up * keep).astype(jnp.bfloat16)
    output = jnp.dot(hidden, down_weight, preferred_element_type=jnp.float32).astype(jnp.bfloat16)
    grad_hidden = jnp.dot(cotangent, down_weight.T, preferred_element_type=jnp.float32) * keep
    sigmoid_gate = jax.nn.sigmoid(gate)
    grad_gate_act = (grad_hidden * up * sigmoid_gate * (1.0 + gate * (1.0 - sigmoid_gate))).astype(jnp.bfloat16)
    grad_up_act = (grad_hidden * gate * sigmoid_gate).astype(jnp.bfloat16)
    grad_scale = 1.0 / math.sqrt(SEQUENCE_TOKENS)
    grad_gate = jnp.dot(tokens.T, grad_gate_act, preferred_element_type=jnp.float32) * grad_scale
    grad_up = jnp.dot(tokens.T, grad_up_act, preferred_element_type=jnp.float32) * grad_scale
    grad_down = jnp.dot(hidden.T, cotangent, preferred_element_type=jnp.float32) * grad_scale
    grad_tokens = (jnp.dot(grad_gate_act, gate_weight.T, preferred_element_type=jnp.float32) + jnp.dot(grad_up_act, up_weight.T, preferred_element_type=jnp.float32)).astype(jnp.bfloat16)
    return (output, grad_tokens, grad_gate, grad_up, grad_down)
```

```python
import functools

import jax
import jax.numpy as jnp
from jax import lax
from jax.experimental import pallas as pl
from jax.experimental.pallas import tpu as pltpu
from jax.sharding import Mesh, PartitionSpec as P

BLK = 128
ROWBLK = 128
KEPT_HEAVY = 7
SEQ = ("x", "zh", "core")
TP = ("zl", "y")
BF16 = jnp.bfloat16
F32 = jnp.float32
ANY = pl.BlockSpec(memory_space=pl.ANY)
VMEM = pl.BlockSpec(memory_space=pltpu.VMEM)
SMEM = pl.BlockSpec(memory_space=pltpu.SMEM)


def nt(a, b):
    return lax.dot_general(a, b, (((1,), (1,)), ((), ())), preferred_element_type=F32)


def nn(a, b):
    return jnp.dot(a, b, preferred_element_type=F32)


def rows_of(r):
    return pl.ds(pl.multiple_of(r * ROWBLK, ROWBLK), ROWBLK)


def blk_of(b):
    return pl.ds(pl.multiple_of(b * BLK, BLK), BLK)


def partials_kernel(capacity, feat, first_ref, masks, own, other, gate_own, gate_other, up_own, up_other,
                    down_own, down_other, out):
    row_blocks, blocks = masks.shape
    first = first_ref[0]

    def pair(k, count):
        r, b = k // blocks, k % blocks
        at = count - first

        @pl.when((masks[r, b] == 1) & (at >= 0) & (at < capacity))
        def _():
            rows, cols = rows_of(r), blk_of(b)
            act = nn(own[rows, :feat], jnp.concatenate([gate_own[:, cols], up_own[:, cols]], axis=1))
            act += nn(other[rows, :feat], jnp.concatenate([gate_other[:, cols], up_other[:, cols]], axis=1))
            grad = nt(own[rows, feat:], down_own[cols, :]) + nt(other[rows, feat:], down_other[cols, :])
            out[rows_of(at), : 2 * BLK] = act.astype(out.dtype)
            out[rows_of(at), 2 * BLK :] = grad.astype(out.dtype)

        return count + masks[r, b]

    total = lax.fori_loop(0, row_blocks * blocks, pair, 0)

    def empty(k, c):
        out[rows_of(k), :] = jnp.zeros((ROWBLK, 3 * BLK), out.dtype)
        return c

    lax.fori_loop(jnp.clip(total - first, 0, capacity), capacity, empty, 0)


def load_acts(core, own, other, acts, sems):
    half = own.shape[0]
    mine = pltpu.make_async_copy(own, acts.at[pl.ds(pl.multiple_of(core * half, half), half)], sems.at[0])
    rest = pltpu.make_async_copy(other, acts.at[pl.ds(pl.multiple_of((1 - core) * half, half), half)], sems.at[1])
    mine.start()
    rest.start()
    mine.wait()
    rest.wait()


def rows_kernel(core_ref, masks, own, other, gate, up, down, out, acts, sems):
    row_blocks, blocks = masks.shape
    feat = down.shape[1]
    load_acts(core_ref[0], own, other, acts, sems)

    def row(r, count):
        def block(b, carry):
            count = carry[0]

            def live(count, fwd, bwd):
                act = acts[rows_of(count), :]
                cols = blk_of(b)
                fwd = fwd + nn(act[:, :BLK], down[cols, :])
                bwd = bwd + nt(act[:, BLK : 2 * BLK], gate[:, cols]) + nt(act[:, 2 * BLK :], up[:, cols])
                return count + 1, fwd, bwd

            return lax.cond(masks[r, b] == 1, live, lambda *c: c, *carry)

        zero = jnp.zeros((ROWBLK, feat), F32)
        count, fwd, bwd = lax.fori_loop(0, blocks, block, (count, zero, zero))
        out[rows_of(r), :feat] = fwd.astype(out.dtype)
        out[rows_of(r), feat:] = bwd.astype(out.dtype)
        return count

    lax.fori_loop(0, row_blocks, row, 0)


def weights_kernel(scale, core_ref, masks, own, other, rows, grad_gate, grad_up, grad_down, acts, turned, where, sems):
    row_blocks, blocks = masks.shape
    feat = grad_down.shape[1]
    b = pl.program_id(0)

    @pl.when(b == 0)
    def _():
        load_acts(core_ref[0], own, other, acts, sems)

        def pair(k, count):
            where[k] = count
            return count + masks[k // blocks, k % blocks]

        lax.fori_loop(0, row_blocks * blocks, pair, 0)
        for r in range(row_blocks):
            turned[:, r * ROWBLK : (r + 1) * ROWBLK] = rows[r * ROWBLK : (r + 1) * ROWBLK, :feat].T

    grad_gate[...] = jnp.zeros_like(grad_gate)
    grad_up[...] = jnp.zeros_like(grad_up)
    grad_down[...] = jnp.zeros_like(grad_down)
    for r in range(row_blocks):

        @pl.when(masks[r, b] == 1)
        def _():
            act = acts[rows_of(where[r * blocks + b]), :]
            both = nn(turned[:, r * ROWBLK : (r + 1) * ROWBLK], act[:, BLK:])
            grad_gate[...] += both[:, :BLK]
            grad_up[...] += both[:, BLK:]
            grad_down[...] += nn(act[:, :BLK].T, rows[r * ROWBLK : (r + 1) * ROWBLK, feat:])

    grad_gate[...] *= scale
    grad_up[...] *= scale
    grad_down[...] *= scale


def copies(array, axis):
    n = lax.axis_size(axis)
    return lax.all_to_all(jnp.broadcast_to(array[None], (n, *array.shape)), axis, 0, 0, tiled=True)


def across(array):
    return lax.ppermute(array, "core", [(0, 1), (1, 0)])


def summed(array, axis):
    n = lax.axis_size(axis)
    tiles = array.reshape(n, array.shape[0] // n, array.shape[1])
    return lax.all_to_all(tiles, axis, 0, 0, tiled=True).astype(F32).sum(axis=0)


def shards(tokens, gate, up, down, masks, cotangent):
    own_rows, feat = tokens.shape
    row_blocks, blocks = masks.shape
    capacity = row_blocks * KEPT_HEAVY
    half = capacity // 2
    core = lax.axis_index("core").astype(jnp.int32)[None]
    params = pltpu.CompilerParams(vmem_limit_bytes=40 << 20)

    gate_other, up_other, down_other = across(gate), across(up), across(down)
    rows = copies(jnp.concatenate([tokens, cotangent], axis=1), TP).reshape(-1, 2 * feat)
    rows_other = across(rows)

    parts = pl.pallas_call(
        functools.partial(partials_kernel, half, feat),
        out_shape=jax.ShapeDtypeStruct((half * ROWBLK, 3 * BLK), BF16),
        in_specs=[SMEM, SMEM] + [VMEM] * 8,
        out_specs=VMEM,
        compiler_params=params,
        name="partials",
    )(core * half, masks, rows, rows_other, gate, gate_other, up, up_other, down, down_other)

    sums = summed(summed(parts, "x"), "zh")
    gate_act, up_act, grad_hidden = sums[:, :BLK], sums[:, BLK : 2 * BLK], sums[:, 2 * BLK :]
    s = jax.nn.sigmoid(gate_act)
    acts = jnp.concatenate(
        [
            (jax.nn.silu(gate_act) * up_act).astype(BF16),
            (grad_hidden * up_act * s * (1.0 + gate_act * (1.0 - s))).astype(BF16),
            (grad_hidden * gate_act * s).astype(BF16),
        ],
        axis=1,
    )
    acts = copies(acts, "zh").reshape(-1, 3 * BLK)
    acts = copies(acts, "x").reshape(-1, 3 * BLK)
    acts_other = across(acts)

    scratch = [pltpu.VMEM((capacity * ROWBLK, 3 * BLK), BF16)]
    partial_rows = pl.pallas_call(
        rows_kernel,
        out_shape=jax.ShapeDtypeStruct((row_blocks * ROWBLK, 2 * feat), BF16),
        in_specs=[SMEM, SMEM, ANY, ANY, VMEM, VMEM, VMEM],
        out_specs=VMEM,
        scratch_shapes=scratch + [pltpu.SemaphoreType.DMA((2,))],
        compiler_params=params,
        name="row_grads",
    )(core, masks, acts, acts_other, gate, up, down)
    out_rows = summed(partial_rows, TP).astype(BF16)

    columns = pl.BlockSpec((feat, BLK), lambda b: (0, b))
    grad_gate, grad_up, grad_down = pl.pallas_call(
        functools.partial(weights_kernel, (row_blocks * ROWBLK) ** -0.5),
        grid=(blocks,),
        out_shape=(
            jax.ShapeDtypeStruct(gate.shape, F32),
            jax.ShapeDtypeStruct(up.shape, F32),
            jax.ShapeDtypeStruct(down.shape, F32),
        ),
        in_specs=[SMEM, SMEM, ANY, ANY, VMEM],
        out_specs=(columns, columns, pl.BlockSpec((BLK, feat), lambda b: (b, 0))),
        scratch_shapes=scratch
        + [
            pltpu.VMEM((feat, row_blocks * ROWBLK), BF16),
            pltpu.SMEM((row_blocks * blocks,), jnp.int32),
            pltpu.SemaphoreType.DMA((2,)),
        ],
        compiler_params=params,
        name="weight_grads",
    )(core, masks, acts, acts_other, rows)
    return out_rows[:, :feat], out_rows[:, feat:], grad_gate, grad_up, grad_down


def solution(mesh):
    fine = Mesh(mesh.devices.reshape(4, 4, 2, 2, 4), SEQ + TP)
    wide, tall = P(SEQ, TP), P(TP, SEQ)
    return jax.shard_map(
        shards,
        mesh=fine,
        in_specs=(tall, wide, wide, tall, P(None, TP), tall),
        out_specs=(tall, tall, wide, wide, tall),
        check_vma=False,
    )
```

```python
import functools

import jax
import jax.numpy as jnp
from jax import lax
from jax.experimental import pallas as pl
from jax.experimental.pallas import tpu as pltpu
from jax.sharding import Mesh, PartitionSpec as P

BLK = 128
ROWBLK = 128
BASE = 3
EXTRA = 4
UNITS = 4
SEQ = ("x", "zh", "core")
TP = ("zl", "y")
BF16 = jnp.bfloat16
F32 = jnp.float32
ANY = pl.BlockSpec(memory_space=pl.ANY)
VMEM = pl.BlockSpec(memory_space=pltpu.VMEM)
SMEM = pl.BlockSpec(memory_space=pltpu.SMEM)
PARAMS = pltpu.CompilerParams(vmem_limit_bytes=40 << 20)


def nt(a, b):
    return lax.dot_general(a, b, (((1,), (1,)), ((), ())), preferred_element_type=F32)


def nn(a, b):
    return jnp.dot(a, b, preferred_element_type=F32)


def tile(i):
    if isinstance(i, int):
        return pl.ds(i * BLK, BLK)
    return pl.ds(pl.multiple_of(i * BLK, BLK), BLK)


class Table:
    def __init__(self, rows, blocks):
        self.rows, self.blocks = rows, blocks
        self.base = 0
        self.extra = self.base + BASE * rows
        self.unit_row = self.extra + EXTRA * rows
        self.row_unit = self.unit_row + rows
        self.live_row = self.row_unit + rows
        self.live_at = self.live_row + rows * blocks
        self.live = self.live_at + rows * blocks
        self.units = self.live + blocks
        self.spare = self.units + 1
        self.size = self.spare + 1
        self.pairs = (BASE + EXTRA) * rows


def table_kernel(t, masks, out):
    def clear(k, c):
        out[k] = 0
        return c

    def none(k, c):
        out[t.live_at + k] = t.pairs
        return c

    lax.fori_loop(0, t.size, clear, 0)
    lax.fori_loop(0, t.rows * t.blocks, none, 0)

    def row(r, units):
        def block(b, count):
            kept = masks[r, b] == 1
            based = count < BASE
            at = jnp.where(based, BASE * r + count, BASE * t.rows + EXTRA * units + count - BASE)
            slot = jnp.where(based, t.base + at, t.extra + at - BASE * t.rows)
            out[jnp.where(kept, slot, t.spare)] = b
            live = t.rows * b + out[t.live + b]
            out[jnp.where(kept, t.live_row + live, t.spare)] = r
            out[jnp.where(kept, t.live_at + live, t.spare)] = at
            out[t.live + b] = out[t.live + b] + masks[r, b]
            return count + masks[r, b]

        count = lax.fori_loop(0, t.blocks, block, 0)
        heavy = count > BASE
        out[t.row_unit + r] = jnp.where(heavy, units, -1)
        out[jnp.where(heavy, t.unit_row + units, t.spare)] = r
        return units + heavy.astype(jnp.int32)

    out[t.units] = lax.fori_loop(0, t.rows, row, 0)


def partials_kernel(t, feat, first_unit, with_base, core_ref, table, own, other, gate_own, gate_other, up_own, up_other,
                    down_own, down_other, out):
    core = core_ref[0]
    before = 0

    def products(at, row, picks):
        rows = tile(row)
        for j, b in enumerate(picks):
            cols = tile(b)
            act = nn(own[rows, :feat], jnp.concatenate([gate_own[:, cols], up_own[:, cols]], axis=1))
            act += nn(other[rows, :feat], jnp.concatenate([gate_other[:, cols], up_other[:, cols]], axis=1))
            grad = nt(own[rows, feat:], down_own[cols, :]) + nt(other[rows, feat:], down_other[cols, :])
            out[tile(at + j), : 2 * BLK] = act.astype(out.dtype)
            out[tile(at + j), 2 * BLK :] = grad.astype(out.dtype)

    if with_base:
        per_core = t.rows // 2
        for i in range(per_core):
            r = core * per_core + i
            products(BASE * i, r, [table[t.base + BASE * r + j] for j in range(BASE)])
        before = BASE * per_core
    per_core = UNITS // 2
    for i in range(per_core):
        u = first_unit + core * per_core + i
        picks = [table[t.extra + EXTRA * u + j] for j in range(EXTRA)]
        products(before + EXTRA * i, table[t.unit_row + u], picks)


def load_acts(t, core, table, halves, acts, sems):
    base, main = BASE * t.rows, BASE * t.rows + EXTRA * UNITS

    def copies_of(moves):
        for k, (ref, skip, at, size, whose) in enumerate(moves):
            start = pl.multiple_of((at + whose * size) * BLK, BLK)
            yield pltpu.make_async_copy(ref.at[pl.ds(skip * BLK, size * BLK)], acts.at[pl.ds(start, size * BLK)], sems.at[k])

    def move(moves):
        for copy in copies_of(moves):
            copy.start()
        for copy in copies_of(moves):
            copy.wait()

    def both(skip, at, size, own, other):
        return [(own, skip, at, size, core), (other, skip, at, size, 1 - core)]

    units = EXTRA * UNITS // 2
    move(both(0, 0, base // 2, *halves[:2]) + both(base // 2, base, units, *halves[:2]))

    @pl.when(table[t.units] > UNITS)
    def _():
        move(both(0, main, units, *halves[2:]))


def rows_kernel(t, core_ref, table, *refs):
    halves, (gate, up, down, out, acts, total, sems) = refs[:4], refs[4:]
    feat = down.shape[1]
    load_acts(t, core_ref[0], table, halves, acts, sems)

    def products(at, picks):
        fwd, bwd = 0.0, 0.0
        for j, b in enumerate(picks):
            act, cols = acts[tile(at + j), :], tile(b)
            fwd += nn(act[:, :BLK], down[cols, :])
            bwd += nt(act[:, BLK:], jnp.concatenate([gate[:, cols], up[:, cols]], axis=1))
        return fwd, bwd

    for r in range(t.rows):
        fwd, bwd = products(BASE * r, [table[t.base + BASE * r + j] for j in range(BASE)])
        total[r, :, :feat] = fwd
        total[r, :, feat:] = bwd
        u = table[t.row_unit + r]

        @pl.when(u >= 0)
        def _():
            fwd, bwd = products(BASE * t.rows + EXTRA * u, [table[t.extra + EXTRA * u + j] for j in range(EXTRA)])
            total[r, :, :feat] += fwd
            total[r, :, feat:] += bwd

    for r in range(t.rows):
        out[tile(r), :] = total[r].astype(out.dtype)


def weights_kernel(t, together, scale, core_ref, table, *refs):
    halves, (rows, grad_gate, grad_up, grad_down, acts, turned, sems) = refs[:4], refs[4:]
    feat = grad_down.shape[1]
    step = pl.program_id(0)

    @pl.when(step == 0)
    def _():
        load_acts(t, core_ref[0], table, halves, acts, sems)
        acts[tile(t.pairs), :] = jnp.zeros((BLK, acts.shape[1]), acts.dtype)
        for r in range(t.rows):
            turned[:, tile(r)] = rows[tile(r), :feat].T

    for i in range(together):
        b = step * together + i

        def two(j):
            live = t.rows * b + j
            picked = [table[t.live_row + live], table[t.live_row + live + 1]]
            act = jnp.concatenate([acts[tile(table[t.live_at + live + k]), :] for k in (0, 1)], axis=0)
            both = nn(jnp.concatenate([turned[:, tile(r)] for r in picked], axis=1), act[:, BLK:])
            cot = jnp.concatenate([rows[tile(r), feat:] for r in picked], axis=0)
            down = nn(act[:, :BLK].T, cot)
            return both[:, :BLK] * scale, both[:, BLK:] * scale, down * scale

        grad_gate[:, tile(i)], grad_up[:, tile(i)], grad_down[tile(i), :] = two(0)
        for j in range(2, t.rows, 2):

            @pl.when(table[t.live + b] > j)
            def _():
                gate, up, down = two(j)
                grad_gate[:, tile(i)] += gate
                grad_up[:, tile(i)] += up
                grad_down[tile(i), :] += down


def copies(array, axis):
    n = lax.axis_size(axis)
    return lax.all_to_all(jnp.broadcast_to(array[None], (n, *array.shape)), axis, 0, 0, tiled=True)


def across(array):
    return lax.ppermute(array, "core", [(0, 1), (1, 0)])


def summed(array, axis):
    n = lax.axis_size(axis)
    tiles = array.reshape(n, array.shape[0] // n, array.shape[1])
    return lax.all_to_all(tiles, axis, 0, 0, tiled=True).astype(F32).sum(axis=0)


def activations(parts):
    sums = summed(summed(parts, "x"), "zh")
    gate, up, grad = sums[:, :BLK], sums[:, BLK : 2 * BLK], sums[:, 2 * BLK :]
    s = jax.nn.sigmoid(gate)
    acts = jnp.concatenate(
        [
            (jax.nn.silu(gate) * up).astype(BF16),
            (grad * up * s * (1.0 + gate * (1.0 - s))).astype(BF16),
            (grad * gate * s).astype(BF16),
        ],
        axis=1,
    )
    acts = copies(acts, "zh").reshape(-1, 3 * BLK)
    acts = copies(acts, "x").reshape(-1, 3 * BLK)
    return acts, across(acts)


def shards(tokens, gate, up, down, masks, cotangent):
    feat = tokens.shape[1]
    row_blocks, blocks = masks.shape
    t = Table(row_blocks, blocks)
    core = lax.axis_index("core").astype(jnp.int32)[None]

    table = pl.pallas_call(
        functools.partial(table_kernel, t),
        out_shape=jax.ShapeDtypeStruct((t.size,), jnp.int32),
        in_specs=[SMEM],
        out_specs=SMEM,
        name="pair_table",
    )(masks)
    heavy_rows = jnp.sum((jnp.sum(masks, axis=1) > BASE).astype(F32))
    crowded = jnp.max(copies(jnp.full((8, 128), heavy_rows), TP)) > UNITS

    gate_other, up_other, down_other = across(gate), across(up), across(down)
    rows = copies(jnp.concatenate([tokens, cotangent], axis=1), TP).reshape(-1, 2 * feat)
    rows_other, crowded = lax.optimization_barrier((across(rows), crowded))

    def partials(first_unit, with_base):
        pairs = BASE * row_blocks // 2 * with_base + EXTRA * UNITS // 2
        return pl.pallas_call(
            functools.partial(partials_kernel, t, feat, first_unit, with_base),
            out_shape=jax.ShapeDtypeStruct((pairs * ROWBLK, 3 * BLK), BF16),
            in_specs=[SMEM, SMEM] + [VMEM] * 8,
            out_specs=VMEM,
            compiler_params=PARAMS,
            name="partials",
        )(core, table, rows, rows_other, gate, gate_other, up, up_other, down, down_other)

    main = activations(partials(0, True))

    def more():
        return activations(partials(UNITS, False))

    def nothing():
        zeros = jnp.zeros((EXTRA * UNITS // 2 * ROWBLK, 3 * BLK), BF16)
        return zeros, zeros

    rest = lax.cond(crowded, more, nothing)
    acts = (*main, *rest)

    scratch = [pltpu.VMEM(((t.pairs + 1) * BLK, 3 * BLK), BF16)]
    partial_rows = pl.pallas_call(
        functools.partial(rows_kernel, t),
        out_shape=jax.ShapeDtypeStruct((row_blocks * ROWBLK, 2 * feat), BF16),
        in_specs=[SMEM, SMEM] + [ANY] * 4 + [VMEM] * 3,
        out_specs=VMEM,
        scratch_shapes=scratch + [pltpu.VMEM((row_blocks, ROWBLK, 2 * feat), F32), pltpu.SemaphoreType.DMA((4,))],
        compiler_params=PARAMS,
        name="row_grads",
    )(core, table, *acts, gate, up, down)
    out_rows = summed(partial_rows, TP).astype(BF16)

    together = 2 if blocks % 2 == 0 else 1
    columns = pl.BlockSpec((feat, together * BLK), lambda b: (0, b))
    grad_gate, grad_up, grad_down = pl.pallas_call(
        functools.partial(weights_kernel, t, together, (row_blocks * ROWBLK) ** -0.5),
        grid=(blocks // together,),
        out_shape=(
            jax.ShapeDtypeStruct(gate.shape, F32),
            jax.ShapeDtypeStruct(up.shape, F32),
            jax.ShapeDtypeStruct(down.shape, F32),
        ),
        in_specs=[SMEM, SMEM] + [ANY] * 4 + [VMEM],
        out_specs=(columns, columns, pl.BlockSpec((together * BLK, feat), lambda b: (b, 0))),
        scratch_shapes=scratch + [pltpu.VMEM((feat, row_blocks * ROWBLK), BF16), pltpu.SemaphoreType.DMA((4,))],
        compiler_params=PARAMS,
        name="weight_grads",
    )(core, table, *acts, rows)
    return out_rows[:, :feat], out_rows[:, feat:], grad_gate, grad_up, grad_down


def solution(mesh):
    fine = Mesh(mesh.devices.reshape(4, 4, 2, 2, 4), SEQ + TP)
    wide, tall = P(SEQ, TP), P(TP, SEQ)
    return jax.shard_map(
        shards,
        mesh=fine,
        in_specs=(tall, wide, wide, tall, P(None, TP), tall),
        out_specs=(tall, tall, wide, wide, tall),
        check_vma=False,
    )
```

```python
import functools

import jax
import jax.numpy as jnp
from jax import lax
from jax.experimental import pallas as pl
from jax.experimental.pallas import tpu as pltpu
from jax.sharding import Mesh, PartitionSpec as P

BLK = 128
ROWBLK = 128
BASE = 3
EXTRA = 4
ROOM = (2, 3, 4, 8)
SEQ = ("x", "zh", "core")
TP = ("zl", "y")
BF16 = jnp.bfloat16
F32 = jnp.float32
ANY = pl.BlockSpec(memory_space=pl.ANY)
VMEM = pl.BlockSpec(memory_space=pltpu.VMEM)
SMEM = pl.BlockSpec(memory_space=pltpu.SMEM)
PARAMS = pltpu.CompilerParams(vmem_limit_bytes=40 << 20)


def nt(a, b):
    return lax.dot_general(a, b, (((1,), (1,)), ((), ())), preferred_element_type=F32)


def nn(a, b):
    return jnp.dot(a, b, preferred_element_type=F32)


def tile(i):
    if isinstance(i, int):
        return pl.ds(i * BLK, BLK)
    return pl.ds(pl.multiple_of(i * BLK, BLK), BLK)


class Table:
    def __init__(self, rows, blocks):
        self.rows, self.blocks = rows, blocks
        self.base = 0
        self.extra = self.base + BASE * rows
        self.unit_row = self.extra + EXTRA * rows
        self.row_unit = self.unit_row + rows
        self.live_row = self.row_unit + rows
        self.live_at = self.live_row + rows * blocks
        self.live = self.live_at + rows * blocks
        self.spare = self.live + blocks
        self.size = self.spare + 1
        self.pairs = (BASE + EXTRA) * rows


def table_kernel(t, masks, out, heavy_rows):
    for k in range(t.extra, t.row_unit):
        out[k] = 0
    for k in range(t.rows * t.blocks):
        out[t.live_row + k] = 0
        out[t.live_at + k] = t.pairs
    units = jnp.int32(0)
    live = [jnp.int32(0)] * t.blocks
    for r in range(t.rows):
        count = jnp.int32(0)
        for b in range(t.blocks):
            one = masks[r, b]
            kept, based = one == 1, count < BASE
            at = jnp.where(based, BASE * r, BASE * (t.rows - 1) + EXTRA * units) + count
            out[jnp.where(kept, t.base + at, t.spare)] = b
            out[jnp.where(kept, t.live_row + t.rows * b + live[b], t.spare)] = r
            out[jnp.where(kept, t.live_at + t.rows * b + live[b], t.spare)] = at
            live[b] += one
            count += one
        heavy = count > BASE
        out[t.row_unit + r] = jnp.where(heavy, units, -1)
        out[jnp.where(heavy, t.unit_row + units, t.spare)] = r
        units += heavy.astype(jnp.int32)
    for b in range(t.blocks):
        out[t.live + b] = live[b]
    heavy_rows[...] = jnp.full(heavy_rows.shape, units.astype(F32))


def partials_kernel(t, units, feat, core_ref, table, own, other, gate_own, gate_other, up_own, up_other, down_own,
                    down_other, out):
    core = core_ref[0]
    base, extra = BASE * t.rows // 2, EXTRA * units // 2

    def products(i, row, block):
        rows, cols = tile(row), tile(block)
        act = nn(own[rows, :feat], jnp.concatenate([gate_own[:, cols], up_own[:, cols]], axis=1))
        act += nn(other[rows, :feat], jnp.concatenate([gate_other[:, cols], up_other[:, cols]], axis=1))
        grad = nt(own[rows, feat:], down_own[cols, :]) + nt(other[rows, feat:], down_other[cols, :])
        out[tile(i), : 2 * BLK] = act.astype(out.dtype)
        out[tile(i), 2 * BLK :] = grad.astype(out.dtype)

    def some_base(n, c):
        for j in range(2 * BASE):
            i = n * 2 * BASE + j
            products(i, core * (t.rows // 2) + n * 2 + j // BASE, table[t.base + core * base + i])
        return c

    def some_extra(n, c):
        for j in range(2):
            i = n * 2 + j
            k = core * extra + i
            products(base + i, table[t.unit_row + k // EXTRA], table[t.extra + k])
        return c

    lax.fori_loop(0, base // (2 * BASE), some_base, 0)
    lax.fori_loop(0, extra // 2, some_extra, 0, unroll=extra // 2 if units <= ROOM[1] else 1)


def load_acts(t, units, core, halves, acts, sems):
    base, extra = BASE * t.rows // 2, EXTRA * units // 2
    moves = []
    for half, whose in zip(halves, (core, 1 - core)):
        for skip, at, size in ((0, 0, base), (base, 2 * base, extra)):
            start = pl.multiple_of((at + whose * size) * BLK, BLK)
            source, target = half.at[pl.ds(skip * BLK, size * BLK)], acts.at[pl.ds(start, size * BLK)]
            moves.append(pltpu.make_async_copy(source, target, sems.at[len(moves)]))
    for move in moves:
        move.start()
    for move in moves:
        move.wait()


def rows_kernel(t, units, core_ref, table, *refs):
    halves, (gate, up, down, out, acts, total, sems) = refs[:2], refs[2:]
    feat = down.shape[1]
    load_acts(t, units, core_ref[0], halves, acts, sems)

    def products(at, picks):
        fwd, bwd = 0.0, 0.0
        for j, b in enumerate(picks):
            act, cols = acts[tile(at + j), :], tile(b)
            fwd += nn(act[:, :BLK], down[cols, :])
            bwd += nt(act[:, BLK:], jnp.concatenate([gate[:, cols], up[:, cols]], axis=1))
        return fwd, bwd

    def row(r, c):
        fwd, bwd = products(BASE * r, [table[t.base + BASE * r + j] for j in range(BASE)])
        total[:, :feat] = fwd
        total[:, feat:] = bwd
        u = table[t.row_unit + r]

        @pl.when(u >= 0)
        def _():
            fwd, bwd = products(BASE * t.rows + EXTRA * u, [table[t.extra + EXTRA * u + j] for j in range(EXTRA)])
            total[:, :feat] += fwd
            total[:, feat:] += bwd

        out[tile(r), :] = total[...].astype(out.dtype)
        return c

    lax.fori_loop(0, t.rows, row, 0)


def weights_kernel(t, units, together, scale, core_ref, table, *refs):
    halves, (rows, grad_gate, grad_up, grad_down, acts, turned, sems) = refs[:2], refs[2:]
    feat = grad_down.shape[1]
    step = pl.program_id(0)

    @pl.when(step == 0)
    def _():
        load_acts(t, units, core_ref[0], halves, acts, sems)
        acts[tile(t.pairs), :] = jnp.zeros((BLK, acts.shape[1]), acts.dtype)
        for r in range(t.rows):
            turned[:, tile(r)] = rows[tile(r), :feat].T

    for i in range(together):
        b = step * together + i

        def two(j):
            live = t.rows * b + j
            picked = [table[t.live_row + live], table[t.live_row + live + 1]]
            act = jnp.concatenate([acts[tile(table[t.live_at + live + k]), :] for k in (0, 1)], axis=0)
            both = nn(jnp.concatenate([turned[:, tile(r)] for r in picked], axis=1), act[:, BLK:])
            cot = jnp.concatenate([rows[tile(r), feat:] for r in picked], axis=0)
            down = nn(act[:, :BLK].T, cot)
            return both[:, :BLK] * scale, both[:, BLK:] * scale, down * scale

        grad_gate[:, tile(i)], grad_up[:, tile(i)], grad_down[tile(i), :] = two(0)
        for j in range(2, t.rows, 2):

            @pl.when(table[t.live + b] > j)
            def _():
                gate, up, down = two(j)
                grad_gate[:, tile(i)] += gate
                grad_up[:, tile(i)] += up
                grad_down[tile(i), :] += down


def copies(array, axis):
    n = lax.axis_size(axis)
    return lax.all_to_all(jnp.broadcast_to(array[None], (n, *array.shape)), axis, 0, 0, tiled=True)


def across(array):
    return lax.ppermute(array, "core", [(0, 1), (1, 0)])


def summed(array, axis):
    n = lax.axis_size(axis)
    tiles = array.reshape(n, array.shape[0] // n, array.shape[1])
    return lax.all_to_all(tiles, axis, 0, 0, tiled=True).astype(F32).sum(axis=0)


def summed_scaled(array, axis):
    n = lax.axis_size(axis)
    size, columns = array.shape[0] // n, array.shape[1]
    peak = jnp.max(jnp.abs(array), axis=0, keepdims=True)
    power = jnp.round(jnp.clip(jnp.log2(jnp.maximum(peak, 1e-36)), -119.0, 119.0))
    tiles = (array * jnp.exp2(-power)).astype(jnp.float16).reshape(n, size, columns)
    powers = jnp.broadcast_to(power.astype(jnp.float16), (n, 16, columns))
    arrived = lax.all_to_all(jnp.concatenate([tiles, powers], axis=1), axis, 0, 0, tiled=True).astype(F32)
    return jnp.sum(arrived[:, :size] * jnp.exp2(arrived[:, size : size + 1]), axis=0)


def activations(parts):
    sums = summed_scaled(summed(parts, "x"), "zh")
    gate, up, grad = sums[:, :BLK], sums[:, BLK : 2 * BLK], sums[:, 2 * BLK :]
    s = jax.nn.sigmoid(gate)
    acts = jnp.concatenate(
        [
            (jax.nn.silu(gate) * up).astype(BF16),
            (grad * up * s * (1.0 + gate * (1.0 - s))).astype(BF16),
            (grad * gate * s).astype(BF16),
        ],
        axis=1,
    )
    acts = copies(acts, "zh").reshape(-1, 3 * BLK)
    acts = copies(acts, "x").reshape(-1, 3 * BLK)
    return acts, across(acts)


def from_rows(units, core, table, rows, rows_other, gate, gate_other, up, up_other, down, down_other, t):
    feat = down.shape[1]
    parts = pl.pallas_call(
        functools.partial(partials_kernel, t, units, feat),
        out_shape=jax.ShapeDtypeStruct(((BASE * t.rows + EXTRA * units) // 2 * ROWBLK, 3 * BLK), BF16),
        in_specs=[SMEM, SMEM] + [VMEM] * 8,
        out_specs=VMEM,
        compiler_params=PARAMS,
        name="partials",
    )(core, table, rows, rows_other, gate, gate_other, up, up_other, down, down_other)
    acts = activations(parts)

    scratch = [pltpu.VMEM(((t.pairs + 1) * BLK, 3 * BLK), BF16)]
    partial_rows = pl.pallas_call(
        functools.partial(rows_kernel, t, units),
        out_shape=jax.ShapeDtypeStruct((t.rows * ROWBLK, 2 * feat), BF16),
        in_specs=[SMEM, SMEM] + [ANY] * 2 + [VMEM] * 3,
        out_specs=VMEM,
        scratch_shapes=scratch + [pltpu.VMEM((ROWBLK, 2 * feat), F32), pltpu.SemaphoreType.DMA((4,))],
        compiler_params=PARAMS,
        name="row_grads",
    )(core, table, *acts, gate, up, down)
    out_rows = summed(partial_rows, TP).astype(BF16)

    together = 2 if t.blocks % 2 == 0 else 1
    columns = pl.BlockSpec((feat, together * BLK), lambda b: (0, b))
    grad_gate, grad_up, grad_down = pl.pallas_call(
        functools.partial(weights_kernel, t, units, together, (t.rows * ROWBLK) ** -0.5),
        grid=(t.blocks // together,),
        out_shape=(
            jax.ShapeDtypeStruct(gate.shape, F32),
            jax.ShapeDtypeStruct(up.shape, F32),
            jax.ShapeDtypeStruct(down.shape, F32),
        ),
        in_specs=[SMEM, SMEM] + [ANY] * 2 + [VMEM],
        out_specs=(columns, columns, pl.BlockSpec((together * BLK, feat), lambda b: (b, 0))),
        scratch_shapes=scratch + [pltpu.VMEM((feat, t.rows * ROWBLK), BF16), pltpu.SemaphoreType.DMA((4,))],
        compiler_params=PARAMS,
        name="weight_grads",
    )(core, table, *acts, rows)
    return out_rows[:, :feat], out_rows[:, feat:], grad_gate, grad_up, grad_down


def shards(tokens, gate, up, down, masks, cotangent):
    feat = tokens.shape[1]
    t = Table(*masks.shape)
    core = lax.axis_index("core").astype(jnp.int32)[None]
    table, heavy_rows = pl.pallas_call(
        functools.partial(table_kernel, t),
        out_shape=(jax.ShapeDtypeStruct((t.size,), jnp.int32), jax.ShapeDtypeStruct((8, 128), F32)),
        in_specs=[SMEM],
        out_specs=(SMEM, VMEM),
        name="pair_table",
    )(masks)
    most = jnp.max(copies(heavy_rows, TP))
    path = sum((most > room).astype(jnp.int32) for room in ROOM[:-1])

    gate_other, up_other, down_other = across(gate), across(up), across(down)
    rows = copies(jnp.concatenate([tokens, cotangent], axis=1), TP).reshape(-1, 2 * feat)
    rows_other = across(rows)
    paths = [functools.partial(from_rows, units, t=t) for units in ROOM]
    return lax.switch(
        path, paths, core, table, rows, rows_other, gate, gate_other, up, up_other, down, down_other
    )


def solution(mesh):
    fine = Mesh(mesh.devices.reshape(4, 4, 2, 2, 4), SEQ + TP)
    wide, tall = P(SEQ, TP), P(TP, SEQ)
    return jax.shard_map(
        shards,
        mesh=fine,
        in_specs=(tall, wide, wide, tall, P(None, TP), tall),
        out_specs=(tall, tall, wide, wide, tall),
        check_vma=False,
    )
```

```python
import functools

import jax
import jax.numpy as jnp
from jax import lax
from jax.experimental import pallas as pl
from jax.experimental.pallas import tpu as pltpu
from jax.sharding import Mesh, PartitionSpec as P

BLK = 128
ROWBLK = 128
BASE = 3
EXTRA = 4
ROOM = (2, 3, 4, 8)
SEQ = ("x", "zh", "core")
TP = ("zl", "y")
BF16 = jnp.bfloat16
F32 = jnp.float32
ANY = pl.BlockSpec(memory_space=pl.ANY)
VMEM = pl.BlockSpec(memory_space=pltpu.VMEM)
SMEM = pl.BlockSpec(memory_space=pltpu.SMEM)
PARAMS = pltpu.CompilerParams(vmem_limit_bytes=40 << 20)


def nt(a, b):
    return lax.dot_general(a, b, (((1,), (1,)), ((), ())), preferred_element_type=F32)


def nn(a, b):
    return jnp.dot(a, b, preferred_element_type=F32)


def tile(i):
    if isinstance(i, int):
        return pl.ds(i * BLK, BLK)
    return pl.ds(pl.multiple_of(i * BLK, BLK), BLK)


class Table:
    def __init__(self, rows, blocks):
        self.rows, self.blocks = rows, blocks
        self.base = 0
        self.extra = self.base + BASE * rows
        self.unit_row = self.extra + EXTRA * rows
        self.row_unit = self.unit_row + rows
        self.live_row = self.row_unit + rows
        self.live_at = self.live_row + rows * blocks
        self.live = self.live_at + rows * blocks
        self.spare = self.live + blocks
        self.size = self.spare + 1
        self.pairs = (BASE + EXTRA) * rows


def payload_kernel(blocks_kept, masks, tokens, cotangent, out):
    rows, feat = tokens.shape
    heavy = jnp.int32(0)
    for r in range(masks.shape[0]):
        kept = sum(masks[r, b] for b in range(masks.shape[1]))
        heavy += (kept > blocks_kept).astype(jnp.int32)
    out[:rows, :feat] = tokens[...]
    out[:rows, feat:] = cotangent[...]
    out[rows:, :] = jnp.full((out.shape[0] - rows, out.shape[1]), heavy.astype(F32)).astype(out.dtype)


def table_kernel(t, masks, out):
    for k in range(t.extra, t.row_unit):
        out[k] = 0
    for k in range(t.rows * t.blocks):
        out[t.live_row + k] = 0
        out[t.live_at + k] = t.pairs
    units = jnp.int32(0)
    live = [jnp.int32(0)] * t.blocks
    for r in range(t.rows):
        count = jnp.int32(0)
        for b in range(t.blocks):
            one = masks[r, b]
            kept, based = one == 1, count < BASE
            at = jnp.where(based, BASE * r, BASE * (t.rows - 1) + EXTRA * units) + count
            out[jnp.where(kept, t.base + at, t.spare)] = b
            out[jnp.where(kept, t.live_row + t.rows * b + live[b], t.spare)] = r
            out[jnp.where(kept, t.live_at + t.rows * b + live[b], t.spare)] = at
            live[b] += one
            count += one
        heavy = count > BASE
        out[t.row_unit + r] = jnp.where(heavy, units, -1)
        out[jnp.where(heavy, t.unit_row + units, t.spare)] = r
        units += heavy.astype(jnp.int32)
    for b in range(t.blocks):
        out[t.live + b] = live[b]


def partials_kernel(t, units, feat, core_ref, table, own, other, gate_own, gate_other, up_own, up_other, down_own,
                    down_other, out):
    core = core_ref[0]
    base, extra = BASE * t.rows // 2, EXTRA * units // 2

    def products(i, row, block):
        cols = tile(block)
        act = nn(own[row, :ROWBLK, :feat], jnp.concatenate([gate_own[:, cols], up_own[:, cols]], axis=1))
        act += nn(other[row, :ROWBLK, :feat], jnp.concatenate([gate_other[:, cols], up_other[:, cols]], axis=1))
        grad = nt(own[row, :ROWBLK, feat:], down_own[cols, :]) + nt(other[row, :ROWBLK, feat:], down_other[cols, :])
        out[tile(i), : 2 * BLK] = act.astype(out.dtype)
        out[tile(i), 2 * BLK :] = grad.astype(out.dtype)

    def some_base(n, c):
        for j in range(2 * BASE):
            i = n * 2 * BASE + j
            products(i, core * (t.rows // 2) + n * 2 + j // BASE, table[t.base + core * base + i])
        return c

    def some_extra(n, c):
        for j in range(2):
            i = n * 2 + j
            k = core * extra + i
            products(base + i, table[t.unit_row + k // EXTRA], table[t.extra + k])
        return c

    lax.fori_loop(0, base // (2 * BASE), some_base, 0)
    lax.fori_loop(0, extra // 2, some_extra, 0, unroll=extra // 2 if units <= ROOM[1] else 1)


def load_acts(t, units, core, halves, acts, sems):
    base, extra = BASE * t.rows // 2, EXTRA * units // 2
    moves = []
    for half, whose in zip(halves, (core, 1 - core)):
        for skip, at, size in ((0, 0, base), (base, 2 * base, extra)):
            start = pl.multiple_of((at + whose * size) * BLK, BLK)
            source, target = half.at[pl.ds(skip * BLK, size * BLK)], acts.at[pl.ds(start, size * BLK)]
            moves.append(pltpu.make_async_copy(source, target, sems.at[len(moves)]))
    for move in moves:
        move.start()
    for move in moves:
        move.wait()


def rows_kernel(t, units, core_ref, table, *refs):
    halves, (gate, up, down, out, acts, total, sems) = refs[:2], refs[2:]
    feat = down.shape[1]
    load_acts(t, units, core_ref[0], halves, acts, sems)

    def products(at, picks):
        fwd, bwd = 0.0, 0.0
        for j, b in enumerate(picks):
            act, cols = acts[tile(at + j), :], tile(b)
            fwd += nn(act[:, :BLK], down[cols, :])
            bwd += nt(act[:, BLK:], jnp.concatenate([gate[:, cols], up[:, cols]], axis=1))
        return fwd, bwd

    def row(r, c):
        fwd, bwd = products(BASE * r, [table[t.base + BASE * r + j] for j in range(BASE)])
        total[:, :feat] = fwd
        total[:, feat:] = bwd
        u = table[t.row_unit + r]

        @pl.when(u >= 0)
        def _():
            fwd, bwd = products(BASE * t.rows + EXTRA * u, [table[t.extra + EXTRA * u + j] for j in range(EXTRA)])
            total[:, :feat] += fwd
            total[:, feat:] += bwd

        out[tile(r), :] = total[...].astype(out.dtype)
        return c

    lax.fori_loop(0, t.rows, row, 0)


def weights_kernel(t, units, together, scale, core_ref, table, *refs):
    halves, (rows, grad_gate, grad_up, grad_down, acts, turned, sems) = refs[:2], refs[2:]
    feat = grad_down.shape[1]
    step = pl.program_id(0)

    @pl.when(step == 0)
    def _():
        load_acts(t, units, core_ref[0], halves, acts, sems)
        acts[tile(t.pairs), :] = jnp.zeros((BLK, acts.shape[1]), acts.dtype)
        for r in range(t.rows):
            turned[:, tile(r)] = rows[r, :ROWBLK, :feat].T

    for i in range(together):
        b = step * together + i

        def two(j):
            live = t.rows * b + j
            picked = [table[t.live_row + live], table[t.live_row + live + 1]]
            act = jnp.concatenate([acts[tile(table[t.live_at + live + k]), :] for k in (0, 1)], axis=0)
            both = nn(jnp.concatenate([turned[:, tile(r)] for r in picked], axis=1), act[:, BLK:])
            cot = jnp.concatenate([rows[r, :ROWBLK, feat:] for r in picked], axis=0)
            down = nn(act[:, :BLK].T, cot)
            return both[:, :BLK] * scale, both[:, BLK:] * scale, down * scale

        grad_gate[:, tile(i)], grad_up[:, tile(i)], grad_down[tile(i), :] = two(0)
        for j in range(2, t.rows, 2):

            @pl.when(table[t.live + b] > j)
            def _():
                gate, up, down = two(j)
                grad_gate[:, tile(i)] += gate
                grad_up[:, tile(i)] += up
                grad_down[tile(i), :] += down


def copies(array, axis):
    n = lax.axis_size(axis)
    return lax.all_to_all(jnp.broadcast_to(array[None], (n, *array.shape)), axis, 0, 0, tiled=True)


def across(array):
    return lax.ppermute(array, "core", [(0, 1), (1, 0)])


def summed(array, axis):
    n = lax.axis_size(axis)
    tiles = array.reshape(n, array.shape[0] // n, array.shape[1])
    return lax.all_to_all(tiles, axis, 0, 0, tiled=True).astype(F32).sum(axis=0)


def summed_scaled(array, axis):
    n = lax.axis_size(axis)
    size, columns = array.shape[0] // n, array.shape[1]
    peak = jnp.max(jnp.abs(array), axis=0, keepdims=True)
    power = jnp.round(jnp.clip(jnp.log2(jnp.maximum(peak, 1e-36)), -119.0, 119.0))
    tiles = (array * jnp.exp2(-power)).astype(jnp.float16).reshape(n, size, columns)
    powers = jnp.broadcast_to(power.astype(jnp.float16), (n, 16, columns))
    arrived = lax.all_to_all(jnp.concatenate([tiles, powers], axis=1), axis, 0, 0, tiled=True).astype(F32)
    return jnp.sum(arrived[:, :size] * jnp.exp2(arrived[:, size : size + 1]), axis=0)


def activations(parts):
    sums = summed_scaled(summed(parts, "x"), "zh")
    gate, up, grad = sums[:, :BLK], sums[:, BLK : 2 * BLK], sums[:, 2 * BLK :]
    s = jax.nn.sigmoid(gate)
    acts = jnp.concatenate(
        [
            (jax.nn.silu(gate) * up).astype(BF16),
            (grad * up * s * (1.0 + gate * (1.0 - s))).astype(BF16),
            (grad * gate * s).astype(BF16),
        ],
        axis=1,
    )
    acts = copies(acts, "zh").reshape(-1, 3 * BLK)
    acts = copies(acts, "x").reshape(-1, 3 * BLK)
    return acts, across(acts)


def from_rows(units, core, table, rows, rows_other, gate, gate_other, up, up_other, down, down_other, t):
    feat = down.shape[1]
    parts = pl.pallas_call(
        functools.partial(partials_kernel, t, units, feat),
        out_shape=jax.ShapeDtypeStruct(((BASE * t.rows + EXTRA * units) // 2 * ROWBLK, 3 * BLK), BF16),
        in_specs=[SMEM, SMEM] + [VMEM] * 8,
        out_specs=VMEM,
        compiler_params=PARAMS,
        name="partials",
    )(core, table, rows, rows_other, gate, gate_other, up, up_other, down, down_other)
    acts = activations(parts)

    scratch = [pltpu.VMEM(((t.pairs + 1) * BLK, 3 * BLK), BF16)]
    partial_rows = pl.pallas_call(
        functools.partial(rows_kernel, t, units),
        out_shape=jax.ShapeDtypeStruct((t.rows * ROWBLK, 2 * feat), BF16),
        in_specs=[SMEM, SMEM] + [ANY] * 2 + [VMEM] * 3,
        out_specs=VMEM,
        scratch_shapes=scratch + [pltpu.VMEM((ROWBLK, 2 * feat), F32), pltpu.SemaphoreType.DMA((4,))],
        compiler_params=PARAMS,
        name="row_grads",
    )(core, table, *acts, gate, up, down)
    out_rows = summed(partial_rows, TP).astype(BF16)

    together = 2 if t.blocks % 2 == 0 else 1
    columns = pl.BlockSpec((feat, together * BLK), lambda b: (0, b))
    grad_gate, grad_up, grad_down = pl.pallas_call(
        functools.partial(weights_kernel, t, units, together, (t.rows * ROWBLK) ** -0.5),
        grid=(t.blocks // together,),
        out_shape=(
            jax.ShapeDtypeStruct(gate.shape, F32),
            jax.ShapeDtypeStruct(up.shape, F32),
            jax.ShapeDtypeStruct(down.shape, F32),
        ),
        in_specs=[SMEM, SMEM] + [ANY] * 2 + [VMEM],
        out_specs=(columns, columns, pl.BlockSpec((together * BLK, feat), lambda b: (b, 0))),
        scratch_shapes=scratch + [pltpu.VMEM((feat, t.rows * ROWBLK), BF16), pltpu.SemaphoreType.DMA((4,))],
        compiler_params=PARAMS,
        name="weight_grads",
    )(core, table, *acts, rows)
    return out_rows[:, :feat], out_rows[:, feat:], grad_gate, grad_up, grad_down


def shards(tokens, gate, up, down, masks, cotangent):
    own_rows, feat = tokens.shape
    t = Table(*masks.shape)
    core = lax.axis_index("core").astype(jnp.int32)[None]
    payload = pl.pallas_call(
        functools.partial(payload_kernel, BASE),
        out_shape=jax.ShapeDtypeStruct((own_rows + 16, 2 * feat), BF16),
        in_specs=[SMEM, VMEM, VMEM],
        out_specs=VMEM,
        name="payload",
    )(masks, tokens, cotangent)
    table = pl.pallas_call(
        functools.partial(table_kernel, t),
        out_shape=jax.ShapeDtypeStruct((t.size,), jnp.int32),
        in_specs=[SMEM],
        out_specs=SMEM,
        name="pair_table",
    )(masks)
    gate_other, up_other, down_other = across(gate), across(up), across(down)
    rows = copies(payload, TP)
    rows, table, gate_other, up_other, down_other = lax.optimization_barrier(
        (rows, table, gate_other, up_other, down_other)
    )
    rows_other = across(rows)
    most = jnp.max(rows[:, own_rows, 0].astype(F32))
    path = sum((most > room).astype(jnp.int32) for room in ROOM[:-1])
    paths = [functools.partial(from_rows, units, t=t) for units in ROOM]
    return lax.switch(
        path, paths, core, table, rows, rows_other, gate, gate_other, up, up_other, down, down_other
    )


def solution(mesh):
    fine = Mesh(mesh.devices.reshape(4, 4, 2, 2, 4), SEQ + TP)
    wide, tall = P(SEQ, TP), P(TP, SEQ)
    return jax.shard_map(
        shards,
        mesh=fine,
        in_specs=(tall, wide, wide, tall, P(None, TP), tall),
        out_specs=(tall, tall, wide, wide, tall),
        check_vma=False,
    )
```

```python
import functools

import jax
import jax.numpy as jnp
from jax import lax
from jax.experimental import pallas as pl
from jax.experimental.pallas import tpu as pltpu
from jax.sharding import Mesh, PartitionSpec as P

BLK = 128
ROWBLK = 128
BASE = 3
EXTRA = 4
ROOM = (2, 3, 8)
SEQ = ("x", "zh", "core")
TP = ("zl", "y")
BF16 = jnp.bfloat16
F32 = jnp.float32
ANY = pl.BlockSpec(memory_space=pl.ANY)
VMEM = pl.BlockSpec(memory_space=pltpu.VMEM)
SMEM = pl.BlockSpec(memory_space=pltpu.SMEM)
PARAMS = pltpu.CompilerParams(vmem_limit_bytes=40 << 20)


def nt(a, b):
    return lax.dot_general(a, b, (((1,), (1,)), ((), ())), preferred_element_type=F32)


def nn(a, b):
    return jnp.dot(a, b, preferred_element_type=F32)


def tile(i):
    if isinstance(i, int):
        return pl.ds(i * BLK, BLK)
    return pl.ds(pl.multiple_of(i * BLK, BLK), BLK)


class Table:
    def __init__(self, rows, blocks):
        self.rows, self.blocks = rows, blocks
        self.base = 0
        self.extra = self.base + BASE * rows
        self.unit_row = self.extra + EXTRA * rows
        self.row_unit = self.unit_row + rows
        self.live_row = self.row_unit + rows
        self.live_at = self.live_row + rows * blocks
        self.live = self.live_at + rows * blocks
        self.spare = self.live + blocks
        self.size = self.spare + 1
        self.pairs = (BASE + EXTRA) * rows


def payload_kernel(blocks_kept, masks, tokens, out):
    rows = tokens.shape[0]
    heavy = jnp.int32(0)
    for r in range(masks.shape[0]):
        kept = sum(masks[r, b] for b in range(masks.shape[1]))
        heavy += (kept > blocks_kept).astype(jnp.int32)
    count = jnp.full((out.shape[1] - rows, out.shape[2]), heavy.astype(F32)).astype(out.dtype)
    for k in range(out.shape[0]):
        out[k, :rows, :] = tokens[...]
        out[k, rows:, :] = count


def cotangent_slot(place, row):
    return (place[1] + 4 - row % 4) % 4 * 2 + (row // 4 + place[2]) % 2


def table_kernel(t, masks, out):
    for k in range(t.extra, t.row_unit):
        out[k] = 0
    for k in range(t.rows * t.blocks):
        out[t.live_row + k] = 0
        out[t.live_at + k] = t.pairs
    units = jnp.int32(0)
    live = [jnp.int32(0)] * t.blocks
    for r in range(t.rows):
        count = jnp.int32(0)
        for b in range(t.blocks):
            one = masks[r, b]
            kept, based = one == 1, count < BASE
            at = jnp.where(based, BASE * r, BASE * (t.rows - 1) + EXTRA * units) + count
            out[jnp.where(kept, t.base + at, t.spare)] = b
            out[jnp.where(kept, t.live_row + t.rows * b + live[b], t.spare)] = r
            out[jnp.where(kept, t.live_at + t.rows * b + live[b], t.spare)] = at
            live[b] += one
            count += one
        heavy = count > BASE
        out[t.row_unit + r] = jnp.where(heavy, units, -1)
        out[jnp.where(heavy, t.unit_row + units, t.spare)] = r
        units += heavy.astype(jnp.int32)
    for b in range(t.blocks):
        out[t.live + b] = live[b]


def for_pairs(t, units, core, table, products):
    base, extra = BASE * t.rows // 2, EXTRA * units // 2

    def some_base(n, c):
        for j in range(2 * BASE):
            i = n * 2 * BASE + j
            products(i, core * (t.rows // 2) + n * 2 + j // BASE, table[t.base + core * base + i])
        return c

    def some_extra(n, c):
        for j in range(2):
            i = n * 2 + j
            k = core * extra + i
            products(base + i, table[t.unit_row + k // EXTRA], table[t.extra + k])
        return c

    lax.fori_loop(0, base // (2 * BASE), some_base, 0)
    lax.fori_loop(0, extra // 2, some_extra, 0, unroll=extra // 2 if units <= 3 else 1)


def gate_up_kernel(t, units, place, table, own, other, gate_own, gate_other, up_own, up_other, out):
    def products(i, row, block):
        cols = tile(block)
        act = nn(own[row, :ROWBLK, :], jnp.concatenate([gate_own[:, cols], up_own[:, cols]], axis=1))
        act += nn(other[row, :ROWBLK, :], jnp.concatenate([gate_other[:, cols], up_other[:, cols]], axis=1))
        out[tile(i), :] = act.astype(out.dtype)

    for_pairs(t, units, place[0], table, products)


def grad_hidden_kernel(t, units, place, table, own, other, down_own, down_other, out):
    def products(i, row, block):
        cols, slot = tile(block), cotangent_slot(place, row)
        grad = nt(own[slot], down_own[cols, :]) + nt(other[slot], down_other[cols, :])
        out[tile(i), :] = grad.astype(out.dtype)

    for_pairs(t, units, place[0], table, products)


def load_acts(t, units, core, halves, acts, sems):
    base, extra = BASE * t.rows // 2, EXTRA * units // 2
    moves = []
    for half, whose in zip(halves, (core, 1 - core)):
        for skip, at, size in ((0, 0, base), (base, 2 * base, extra)):
            start = pl.multiple_of((at + whose * size) * BLK, BLK)
            source, target = half.at[pl.ds(skip * BLK, size * BLK)], acts.at[pl.ds(start, size * BLK)]
            moves.append(pltpu.make_async_copy(source, target, sems.at[len(moves)]))
    for move in moves:
        move.start()
    for move in moves:
        move.wait()


def rows_kernel(t, units, place, table, *refs):
    halves, (gate, up, down, out, acts, total, sems) = refs[:2], refs[2:]
    feat = down.shape[1]
    load_acts(t, units, place[0], halves, acts, sems)

    def products(at, picks):
        fwd, bwd = 0.0, 0.0
        for j, b in enumerate(picks):
            act, cols = acts[tile(at + j), :], tile(b)
            fwd += nn(act[:, :BLK], down[cols, :])
            bwd += nt(act[:, BLK:], jnp.concatenate([gate[:, cols], up[:, cols]], axis=1))
        return fwd, bwd

    def row(r, c):
        fwd, bwd = products(BASE * r, [table[t.base + BASE * r + j] for j in range(BASE)])
        total[:, :feat] = fwd
        total[:, feat:] = bwd
        u = table[t.row_unit + r]

        @pl.when(u >= 0)
        def _():
            fwd, bwd = products(BASE * t.rows + EXTRA * u, [table[t.extra + EXTRA * u + j] for j in range(EXTRA)])
            total[:, :feat] += fwd
            total[:, feat:] += bwd

        out[tile(r), :] = total[...].astype(out.dtype)
        return c

    lax.fori_loop(0, t.rows, row, 0)


def weights_kernel(t, units, together, scale, place, table, *refs):
    halves, (rows, cotangent, grad_gate, grad_up, grad_down, acts, turned, sems) = refs[:2], refs[2:]
    step = pl.program_id(0)

    @pl.when(step == 0)
    def _():
        load_acts(t, units, place[0], halves, acts, sems)
        acts[tile(t.pairs), :] = jnp.zeros((BLK, acts.shape[1]), acts.dtype)
        for r in range(t.rows):
            turned[:, tile(r)] = rows[r, :ROWBLK, :].T

    for ref in (grad_gate, grad_up, grad_down):
        ref[...] = jnp.zeros_like(ref)

    def block(i, c):
        b = step * together + i

        def two(j, c):
            live = t.rows * b + 2 * j
            picked = [table[t.live_row + live], table[t.live_row + live + 1]]
            act = jnp.concatenate([acts[tile(table[t.live_at + live + k]), :] for k in (0, 1)], axis=0)
            both = nn(jnp.concatenate([turned[:, tile(r)] for r in picked], axis=1), act[:, BLK:]) * scale
            cot = jnp.concatenate([cotangent[cotangent_slot(place, r)] for r in picked], axis=0)
            grad_gate[:, tile(i)] += both[:, :BLK]
            grad_up[:, tile(i)] += both[:, BLK:]
            grad_down[tile(i), :] += nn(act[:, :BLK].T, cot) * scale
            return c

        return lax.fori_loop(0, (table[t.live + b] + 1) // 2, two, c)

    lax.fori_loop(0, together, block, 0)


def copies(array, axis):
    n = lax.axis_size(axis)
    return lax.all_to_all(jnp.broadcast_to(array[None], (n, *array.shape)), axis, 0, 0, tiled=True)


def across(array):
    return lax.ppermute(array, "core", [(0, 1), (1, 0)])


def moved(array, axis):
    n = lax.axis_size(axis)
    tiles = array.reshape(n, array.shape[0] // n, array.shape[1])
    return lax.all_to_all(tiles, axis, 0, 0, tiled=True)


def summed(array, axis):
    return moved(array, axis).astype(F32).sum(axis=0)


def summed_scaled(array, axis):
    n = lax.axis_size(axis)
    size, columns = array.shape[0] // n, array.shape[1]
    peak = jnp.max(jnp.abs(array), axis=0, keepdims=True)
    power = jnp.round(jnp.clip(jnp.log2(jnp.maximum(peak, 1e-36)), -119.0, 119.0))
    tiles = (array * jnp.exp2(-power)).astype(jnp.float16).reshape(n, size, columns)
    powers = jnp.broadcast_to(power.astype(jnp.float16), (n, 16, columns))
    arrived = lax.all_to_all(jnp.concatenate([tiles, powers], axis=1), axis, 0, 0, tiled=True).astype(F32)
    return jnp.sum(arrived[:, :size] * jnp.exp2(arrived[:, size : size + 1]), axis=0)


def activations(sums):
    sums = summed_scaled(sums, "zh")
    gate, up, grad = sums[:, :BLK], sums[:, BLK : 2 * BLK], sums[:, 2 * BLK :]
    s = jax.nn.sigmoid(gate)
    acts = jnp.concatenate(
        [
            (jax.nn.silu(gate) * up).astype(BF16),
            (grad * up * s * (1.0 + gate * (1.0 - s))).astype(BF16),
            (grad * gate * s).astype(BF16),
        ],
        axis=1,
    )
    acts = copies(acts, "zh").reshape(-1, 3 * BLK)
    acts = copies(acts, "x").reshape(-1, 3 * BLK)
    return acts, across(acts)


def along_y(array):
    n = lax.axis_size("y")
    moved = [lax.ppermute(array, "y", [(i, (i + d) % n) for i in range(n)]) for d in range(1, n)]
    return jnp.concatenate([array] + moved, axis=0)


def from_rows(units, place, table, rows, rows_other, cotangent, gate, gate_other, up, up_other, down, down_other, t):
    feat = down.shape[1]
    pairs = (BASE * t.rows + EXTRA * units) // 2
    gate_up = pl.pallas_call(
        functools.partial(gate_up_kernel, t, units),
        out_shape=jax.ShapeDtypeStruct((pairs * ROWBLK, 2 * BLK), BF16),
        in_specs=[SMEM, SMEM] + [VMEM] * 6,
        out_specs=VMEM,
        compiler_params=PARAMS,
        name="gate_up",
    )(place, table, rows, rows_other, gate, gate_other, up, up_other)
    cotangent = along_y(cotangent).reshape(t.rows, ROWBLK, feat)
    grad_hidden = pl.pallas_call(
        functools.partial(grad_hidden_kernel, t, units),
        out_shape=jax.ShapeDtypeStruct((pairs * ROWBLK, BLK), BF16),
        in_specs=[SMEM, SMEM] + [VMEM] * 4,
        out_specs=VMEM,
        compiler_params=PARAMS,
        name="grad_hidden",
    )(place, table, cotangent, across(cotangent), down, down_other)
    arrived, grad_hidden = lax.optimization_barrier((moved(gate_up, "x"), grad_hidden))
    sums = [jnp.sum(part.astype(F32), axis=0) for part in (arrived, moved(grad_hidden, "x"))]
    acts = activations(jnp.concatenate(sums, axis=1))

    scratch = [pltpu.VMEM(((t.pairs + 1) * BLK, 3 * BLK), BF16)]
    partial_rows = pl.pallas_call(
        functools.partial(rows_kernel, t, units),
        out_shape=jax.ShapeDtypeStruct((t.rows * ROWBLK, 2 * feat), BF16),
        in_specs=[SMEM, SMEM] + [ANY] * 2 + [VMEM] * 3,
        out_specs=VMEM,
        scratch_shapes=scratch + [pltpu.VMEM((ROWBLK, 2 * feat), F32), pltpu.SemaphoreType.DMA((4,))],
        compiler_params=PARAMS,
        name="row_grads",
    )(place, table, *acts, gate, up, down)
    out_rows = summed(partial_rows, TP).astype(BF16)

    together = 2 if t.blocks % 2 == 0 else 1
    columns = pl.BlockSpec((feat, together * BLK), lambda b: (0, b))
    grad_gate, grad_up, grad_down = pl.pallas_call(
        functools.partial(weights_kernel, t, units, together, (t.rows * ROWBLK) ** -0.5),
        grid=(t.blocks // together,),
        out_shape=(
            jax.ShapeDtypeStruct(gate.shape, F32),
            jax.ShapeDtypeStruct(up.shape, F32),
            jax.ShapeDtypeStruct(down.shape, F32),
        ),
        in_specs=[SMEM, SMEM] + [ANY] * 2 + [VMEM] * 2,
        out_specs=(columns, columns, pl.BlockSpec((together * BLK, feat), lambda b: (b, 0))),
        scratch_shapes=scratch + [pltpu.VMEM((feat, t.rows * ROWBLK), BF16), pltpu.SemaphoreType.DMA((4,))],
        compiler_params=PARAMS,
        name="weight_grads",
    )(place, table, *acts, rows, cotangent)
    return out_rows[:, :feat], out_rows[:, feat:], grad_gate, grad_up, grad_down


def shards(tokens, gate, up, down, masks, cotangent):
    own_rows, feat = tokens.shape
    t = Table(*masks.shape)
    place = jnp.stack([lax.axis_index(axis) for axis in ("core", "y", "zl")]).astype(jnp.int32)
    payload = pl.pallas_call(
        functools.partial(payload_kernel, BASE),
        out_shape=jax.ShapeDtypeStruct((lax.axis_size(TP), own_rows + 16, feat), BF16),
        in_specs=[SMEM, VMEM],
        out_specs=VMEM,
        name="payload",
    )(masks, tokens)
    table = pl.pallas_call(
        functools.partial(table_kernel, t),
        out_shape=jax.ShapeDtypeStruct((t.size,), jnp.int32),
        in_specs=[SMEM],
        out_specs=SMEM,
        name="pair_table",
    )(masks)
    gate_other, up_other, down_other = across(gate), across(up), across(down)
    rows = lax.all_to_all(payload, TP, 0, 0, tiled=True)
    cotangents = jnp.concatenate([cotangent, lax.ppermute(cotangent, "zl", [(0, 1), (1, 0)])], axis=0)
    rows, table, cotangents, gate_other, up_other, down_other = lax.optimization_barrier(
        (rows, table, cotangents, gate_other, up_other, down_other)
    )
    rows_other = across(rows)
    most = jnp.max(rows[:, own_rows, 0].astype(F32))
    path = sum((most > room).astype(jnp.int32) for room in ROOM[:-1])
    paths = [functools.partial(from_rows, units, t=t) for units in ROOM]
    return lax.switch(
        path, paths, place, table, rows, rows_other, cotangents, gate, gate_other, up, up_other, down, down_other
    )


def solution(mesh):
    fine = Mesh(mesh.devices.reshape(4, 4, 2, 2, 4), SEQ + TP)
    wide, tall = P(SEQ, TP), P(TP, SEQ)
    return jax.shard_map(
        shards,
        mesh=fine,
        in_specs=(tall, wide, wide, tall, P(None, TP), tall),
        out_specs=(tall, tall, wide, wide, tall),
        check_vma=False,
    )
```

```python
import functools

import jax
import jax.numpy as jnp
from jax import lax
from jax.experimental import pallas as pl
from jax.experimental.pallas import tpu as pltpu
from jax.sharding import Mesh, PartitionSpec as P

BLK = 128
ROWBLK = 128
BASE = 3
EXTRA = 4
ROOM = (2, 3, 8)
SEQ = ("x", "zh", "core")
TP = ("zl", "y")
BF16 = jnp.bfloat16
F32 = jnp.float32
ANY = pl.BlockSpec(memory_space=pl.ANY)
VMEM = pl.BlockSpec(memory_space=pltpu.VMEM)
SMEM = pl.BlockSpec(memory_space=pltpu.SMEM)
PARAMS = pltpu.CompilerParams(vmem_limit_bytes=40 << 20)


def nt(a, b):
    return lax.dot_general(a, b, (((1,), (1,)), ((), ())), preferred_element_type=F32)


def nn(a, b):
    return jnp.dot(a, b, preferred_element_type=F32)


def tile(i):
    if isinstance(i, int):
        return pl.ds(i * BLK, BLK)
    return pl.ds(pl.multiple_of(i * BLK, BLK), BLK)


class Table:
    def __init__(self, rows, blocks):
        self.rows, self.blocks = rows, blocks
        self.base = 0
        self.extra = self.base + BASE * rows
        self.unit_row = self.extra + EXTRA * rows
        self.row_unit = self.unit_row + rows
        self.live_row = self.row_unit + rows
        self.live_at = self.live_row + rows * blocks
        self.live = self.live_at + rows * blocks
        self.spare = self.live + blocks
        self.size = self.spare + 1
        self.pairs = (BASE + EXTRA) * rows


def payload_kernel(blocks_kept, masks, tokens, cotangent, out):
    rows, feat = tokens.shape
    heavy = jnp.int32(0)
    for r in range(masks.shape[0]):
        kept = sum(masks[r, b] for b in range(masks.shape[1]))
        heavy += (kept > blocks_kept).astype(jnp.int32)
    count = jnp.full((out.shape[1] - rows, out.shape[2]), heavy.astype(F32)).astype(out.dtype)
    for k in range(out.shape[0]):
        out[k, :rows, :feat] = tokens[...]
        out[k, :rows, feat:] = cotangent[...]
        out[k, rows:, :] = count


def table_kernel(t, masks, out):
    for k in range(t.extra, t.row_unit):
        out[k] = 0
    for k in range(t.rows * t.blocks):
        out[t.live_row + k] = 0
        out[t.live_at + k] = t.pairs
    units = jnp.int32(0)
    live = [jnp.int32(0)] * t.blocks
    for r in range(t.rows):
        count = jnp.int32(0)
        for b in range(t.blocks):
            one = masks[r, b]
            kept, based = one == 1, count < BASE
            at = jnp.where(based, BASE * r, BASE * (t.rows - 1) + EXTRA * units) + count
            out[jnp.where(kept, t.base + at, t.spare)] = b
            out[jnp.where(kept, t.live_row + t.rows * b + live[b], t.spare)] = r
            out[jnp.where(kept, t.live_at + t.rows * b + live[b], t.spare)] = at
            live[b] += one
            count += one
        heavy = count > BASE
        out[t.row_unit + r] = jnp.where(heavy, units, -1)
        out[jnp.where(heavy, t.unit_row + units, t.spare)] = r
        units += heavy.astype(jnp.int32)
    for b in range(t.blocks):
        out[t.live + b] = live[b]


def partials_kernel(t, units, feat, place, table, own, other, gate_own, gate_other, up_own, up_other, down_own,
                    down_other, out):
    core = place[0]
    base, extra = BASE * t.rows // 2, EXTRA * units // 2

    def products(i, row, block):
        cols = tile(block)
        act = nn(own[row, :ROWBLK, :feat], jnp.concatenate([gate_own[:, cols], up_own[:, cols]], axis=1))
        act += nn(other[row, :ROWBLK, :feat], jnp.concatenate([gate_other[:, cols], up_other[:, cols]], axis=1))
        grad = nt(own[row, :ROWBLK, feat:], down_own[cols, :]) + nt(other[row, :ROWBLK, feat:], down_other[cols, :])
        out[tile(i), : 2 * BLK] = act.astype(out.dtype)
        out[tile(i), 2 * BLK :] = grad.astype(out.dtype)

    def some_base(n, c):
        for j in range(2 * BASE):
            i = n * 2 * BASE + j
            products(i, core * (t.rows // 2) + n * 2 + j // BASE, table[t.base + core * base + i])
        return c

    def some_extra(n, c):
        for j in range(2):
            i = n * 2 + j
            k = core * extra + i
            products(base + i, table[t.unit_row + k // EXTRA], table[t.extra + k])
        return c

    lax.fori_loop(0, base // (2 * BASE), some_base, 0)
    lax.fori_loop(0, extra // 2, some_extra, 0, unroll=extra // 2 if units <= 3 else 1)


def listed(t, units, at):
    base, extra = BASE * t.rows // 2, EXTRA * units // 2
    e = at - 2 * base
    in_base = at + jnp.where(at >= base, extra, 0)
    return jnp.where(e < 0, in_base, base + e + jnp.where(e >= extra, base, 0))


def load_acts(t, units, place, blocks, acts, sems):
    quarter = (BASE * t.rows + EXTRA * units) * BLK // 8
    core, x = place[0], place[1]
    moves = []
    for k, whose in enumerate((core, 1 - core)):
        own, near, far = blocks[3 * k : 3 * k + 3]
        for ref, skip, d in ((own, 0, 0), (near, 0, 3), (near, quarter, 1), (far, 0, 2)):
            start = pl.multiple_of((4 * whose + (x + d) % 4) * quarter, 16)
            source, target = ref.at[pl.ds(skip, quarter)], acts.at[pl.ds(start, quarter)]
            moves.append(pltpu.make_async_copy(source, target, sems.at[len(moves)]))
    for move in moves:
        move.start()
    for move in moves:
        move.wait()


def rows_kernel(t, units, place, table, *refs):
    halves, (gate, up, down, out, acts, total, done, sems) = refs[:6], refs[6:]
    feat = down.shape[1]
    load_acts(t, units, place, halves, acts, sems)

    def products(at, picks):
        fwd, bwd = 0.0, 0.0
        for j, b in enumerate(picks):
            act, cols = acts[tile(listed(t, units, at + j)), :], tile(b)
            fwd += nn(act[:, :BLK], down[cols, :])
            bwd += nt(act[:, BLK:], jnp.concatenate([gate[:, cols], up[:, cols]], axis=1))
        return fwd, bwd

    def row(r, c):
        fwd, bwd = products(BASE * r, [table[t.base + BASE * r + j] for j in range(BASE)])
        total[:, :feat] = fwd
        total[:, feat:] = bwd
        u = table[t.row_unit + r]

        @pl.when(u >= 0)
        def _():
            fwd, bwd = products(BASE * t.rows + EXTRA * u, [table[t.extra + EXTRA * u + j] for j in range(EXTRA)])
            total[:, :feat] += fwd
            total[:, feat:] += bwd

        done[tile(r), :] = total[...].astype(done.dtype)
        pltpu.make_async_copy(done.at[tile(r)], out.at[tile(r)], sems.at[8]).start()
        return c

    lax.fori_loop(0, t.rows, row, 0)
    pltpu.make_async_copy(done, out, sems.at[8]).wait()


def weights_kernel(t, units, together, scale, place, table, *refs):
    halves, (rows, grad_gate, grad_up, grad_down, acts, turned, sems) = refs[:6], refs[6:]
    feat = grad_down.shape[1]
    step = pl.program_id(0)

    @pl.when(step == 0)
    def _():
        load_acts(t, units, place, halves, acts, sems)
        acts[tile(t.pairs), :] = jnp.zeros((BLK, acts.shape[1]), acts.dtype)
        for r in range(t.rows):
            turned[:, tile(r)] = rows[r, :ROWBLK, :feat].T

    for ref in (grad_gate, grad_up, grad_down):
        ref[...] = jnp.zeros_like(ref)

    def block(i, c):
        b = step * together + i

        def two(j, c):
            live = t.rows * b + 2 * j
            picked = [table[t.live_row + live], table[t.live_row + live + 1]]
            act = jnp.concatenate([acts[tile(listed(t, units, table[t.live_at + live + k])), :] for k in (0, 1)], axis=0)
            both = nn(jnp.concatenate([turned[:, tile(r)] for r in picked], axis=1), act[:, BLK:]) * scale
            cot = jnp.concatenate([rows[r, :ROWBLK, feat:] for r in picked], axis=0)
            grad_gate[:, tile(i)] += both[:, :BLK]
            grad_up[:, tile(i)] += both[:, BLK:]
            grad_down[tile(i), :] += nn(act[:, :BLK].T, cot) * scale
            return c

        return lax.fori_loop(0, (table[t.live + b] + 1) // 2, two, c)

    lax.fori_loop(0, together, block, 0)


def copies(array, axis):
    n = lax.axis_size(axis)
    return lax.all_to_all(jnp.broadcast_to(array[None], (n, *array.shape)), axis, 0, 0, tiled=True)


def across(array):
    return lax.ppermute(array, "core", [(0, 1), (1, 0)])


def onward(array, d):
    n = lax.axis_size("x")
    return lax.ppermute(array, "x", [(i, (i + d) % n) for i in range(n)])


def summed(array, axis):
    n = lax.axis_size(axis)
    tiles = array.reshape(n, array.shape[0] // n, array.shape[1])
    return lax.all_to_all(tiles, axis, 0, 0, tiled=True).astype(F32).sum(axis=0)


def summed_scaled(array, axis):
    n = lax.axis_size(axis)
    size, columns = array.shape[0] // n, array.shape[1]
    peak = jnp.max(jnp.abs(array), axis=0, keepdims=True)
    power = jnp.round(jnp.clip(jnp.log2(jnp.maximum(peak, 1e-36)), -119.0, 119.0))
    tiles = (array * jnp.exp2(-power)).astype(jnp.float16).reshape(n, size, columns)
    powers = jnp.broadcast_to(power.astype(jnp.float16), (n, 16, columns))
    arrived = lax.all_to_all(jnp.concatenate([tiles, powers], axis=1), axis, 0, 0, tiled=True).astype(F32)
    return jnp.sum(arrived[:, :size] * jnp.exp2(arrived[:, size : size + 1]), axis=0)


def activations(parts):
    sums = summed_scaled(summed(parts, "x"), "zh")
    gate, up, grad = sums[:, :BLK], sums[:, BLK : 2 * BLK], sums[:, 2 * BLK :]
    s = jax.nn.sigmoid(gate)
    acts = jnp.concatenate(
        [
            (jax.nn.silu(gate) * up).astype(BF16),
            (grad * up * s * (1.0 + gate * (1.0 - s))).astype(BF16),
            (grad * gate * s).astype(BF16),
        ],
        axis=1,
    )
    own = copies(acts, "zh").reshape(-1, 3 * BLK)
    half = own.shape[0] // 2
    before, after = onward(own, 1), onward(own, -1)
    far = jnp.concatenate([onward(before[:half], 1), onward(after[half:], -1)], axis=0)
    blocks = own, jnp.concatenate([before, after], axis=0), far
    return *blocks, *map(across, blocks)


def from_rows(units, place, table, rows, rows_other, gate, gate_other, up, up_other, down, down_other, t):
    feat = down.shape[1]
    parts = pl.pallas_call(
        functools.partial(partials_kernel, t, units, feat),
        out_shape=jax.ShapeDtypeStruct(((BASE * t.rows + EXTRA * units) // 2 * ROWBLK, 3 * BLK), BF16),
        in_specs=[SMEM, SMEM] + [VMEM] * 8,
        out_specs=VMEM,
        compiler_params=PARAMS,
        name="partials",
    )(place, table, rows, rows_other, gate, gate_other, up, up_other, down, down_other)
    acts = activations(parts)

    scratch = [pltpu.VMEM(((t.pairs + 1) * BLK, 3 * BLK), BF16)]
    partial_rows = pl.pallas_call(
        functools.partial(rows_kernel, t, units),
        out_shape=jax.ShapeDtypeStruct((t.rows * ROWBLK, 2 * feat), BF16),
        in_specs=[SMEM, SMEM] + [ANY] * 6 + [VMEM] * 3,
        out_specs=pl.BlockSpec(memory_space=pltpu.HBM),
        scratch_shapes=scratch
        + [
            pltpu.VMEM((ROWBLK, 2 * feat), F32),
            pltpu.VMEM((t.rows * ROWBLK, 2 * feat), BF16),
            pltpu.SemaphoreType.DMA((9,)),
        ],
        compiler_params=PARAMS,
        name="row_grads",
    )(place, table, *acts, gate, up, down)
    out_rows = summed(partial_rows, TP).astype(BF16)

    together = 2 if t.blocks % 2 == 0 else 1
    columns = pl.BlockSpec((feat, together * BLK), lambda b: (0, b))
    grad_gate, grad_up, grad_down = pl.pallas_call(
        functools.partial(weights_kernel, t, units, together, (t.rows * ROWBLK) ** -0.5),
        grid=(t.blocks // together,),
        out_shape=(
            jax.ShapeDtypeStruct(gate.shape, F32),
            jax.ShapeDtypeStruct(up.shape, F32),
            jax.ShapeDtypeStruct(down.shape, F32),
        ),
        in_specs=[SMEM, SMEM] + [ANY] * 6 + [VMEM],
        out_specs=(columns, columns, pl.BlockSpec((together * BLK, feat), lambda b: (b, 0))),
        scratch_shapes=scratch + [pltpu.VMEM((feat, t.rows * ROWBLK), BF16), pltpu.SemaphoreType.DMA((8,))],
        compiler_params=PARAMS,
        name="weight_grads",
    )(place, table, *acts, rows)
    return out_rows[:, :feat], out_rows[:, feat:], grad_gate, grad_up, grad_down


def shards(tokens, gate, up, down, masks, cotangent):
    own_rows, feat = tokens.shape
    t = Table(*masks.shape)
    place = jnp.stack([lax.axis_index("core"), lax.axis_index("x")]).astype(jnp.int32)
    payload = pl.pallas_call(
        functools.partial(payload_kernel, BASE),
        out_shape=jax.ShapeDtypeStruct((lax.axis_size(TP), own_rows + 16, 2 * feat), BF16),
        in_specs=[SMEM, VMEM, VMEM],
        out_specs=VMEM,
        name="payload",
    )(masks, tokens, cotangent)
    table = pl.pallas_call(
        functools.partial(table_kernel, t),
        out_shape=jax.ShapeDtypeStruct((t.size,), jnp.int32),
        in_specs=[SMEM],
        out_specs=SMEM,
        name="pair_table",
    )(masks)
    gate_other, up_other, down_other = across(gate), across(up), across(down)
    rows = lax.all_to_all(payload, TP, 0, 0, tiled=True)
    rows, table, gate_other, up_other, down_other = lax.optimization_barrier(
        (rows, table, gate_other, up_other, down_other)
    )
    rows_other = across(rows)
    most = jnp.max(rows[:, own_rows, 0].astype(F32))
    path = sum((most > room).astype(jnp.int32) for room in ROOM[:-1])
    paths = [functools.partial(from_rows, units, t=t) for units in ROOM]
    return lax.switch(
        path, paths, place, table, rows, rows_other, gate, gate_other, up, up_other, down, down_other
    )


def solution(mesh):
    fine = Mesh(mesh.devices.reshape(4, 4, 2, 2, 4), SEQ + TP)
    wide, tall = P(SEQ, TP), P(TP, SEQ)
    return jax.shard_map(
        shards,
        mesh=fine,
        in_specs=(tall, wide, wide, tall, P(None, TP), tall),
        out_specs=(tall, tall, wide, wide, tall),
        check_vma=False,
    )
```

```python
import functools

import jax
import jax.numpy as jnp
from jax import lax
from jax.experimental import pallas as pl
from jax.experimental.pallas import tpu as pltpu
from jax.sharding import Mesh, PartitionSpec as P

BLK = 128
ROWBLK = 128
BASE = 3
EXTRA = 4
ROOM = (2, 3, 8)
SEQ = ("x", "zh", "core")
TP = ("zl", "y")
BF16 = jnp.bfloat16
F32 = jnp.float32
ANY = pl.BlockSpec(memory_space=pl.ANY)
VMEM = pl.BlockSpec(memory_space=pltpu.VMEM)
SMEM = pl.BlockSpec(memory_space=pltpu.SMEM)
PARAMS = pltpu.CompilerParams(vmem_limit_bytes=40 << 20)


def nt(a, b):
    return lax.dot_general(a, b, (((1,), (1,)), ((), ())), preferred_element_type=F32)


def nn(a, b):
    return jnp.dot(a, b, preferred_element_type=F32)


def tile(i):
    if isinstance(i, int):
        return pl.ds(i * BLK, BLK)
    return pl.ds(pl.multiple_of(i * BLK, BLK), BLK)


class Table:
    def __init__(self, rows, blocks):
        self.rows, self.blocks = rows, blocks
        self.base = 0
        self.extra = self.base + BASE * rows
        self.unit_row = self.extra + EXTRA * rows
        self.row_unit = self.unit_row + rows
        self.live_row = self.row_unit + rows
        self.live_at = self.live_row + rows * blocks
        self.live = self.live_at + rows * blocks
        self.spare = self.live + blocks
        self.size = self.spare + 1
        self.pairs = (BASE + EXTRA) * rows


def payload_kernel(blocks_kept, masks, tokens, cotangent, out):
    rows, feat = tokens.shape
    heavy = jnp.int32(0)
    for r in range(masks.shape[0]):
        kept = sum(masks[r, b] for b in range(masks.shape[1]))
        heavy += (kept > blocks_kept).astype(jnp.int32)
    count = jnp.full((out.shape[1] - rows, out.shape[2]), heavy.astype(F32)).astype(out.dtype)
    for k in range(out.shape[0]):
        out[k, :rows, :feat] = tokens[...]
        out[k, :rows, feat:] = cotangent[...]
        out[k, rows:, :] = count


def table_kernel(t, masks, out):
    for k in range(t.extra, t.row_unit):
        out[k] = 0
    for k in range(t.rows * t.blocks):
        out[t.live_row + k] = 0
        out[t.live_at + k] = t.pairs

    def row(r, c):
        units, live = c[0], list(c[1:])
        count = jnp.int32(0)
        for b in range(t.blocks):
            one = masks[r, b]
            kept, based = one == 1, count < BASE
            at = jnp.where(based, BASE * r, BASE * (t.rows - 1) + EXTRA * units) + count
            out[jnp.where(kept, t.base + at, t.spare)] = b
            out[jnp.where(kept, t.live_row + t.rows * b + live[b], t.spare)] = r
            out[jnp.where(kept, t.live_at + t.rows * b + live[b], t.spare)] = at
            live[b] += one
            count += one
        heavy = count > BASE
        out[t.row_unit + r] = jnp.where(heavy, units, -1)
        out[jnp.where(heavy, t.unit_row + units, t.spare)] = r
        return units + heavy.astype(jnp.int32), *live

    _, *live = lax.fori_loop(0, t.rows, row, (jnp.int32(0),) * (t.blocks + 1))
    for b in range(t.blocks):
        out[t.live + b] = live[b]


def partials_kernel(t, units, feat, place, table, own, other, gate_own, gate_other, up_own, up_other, down_own,
                    down_other, out):
    core = place[0]
    base, extra = BASE * t.rows // 2, EXTRA * units // 2

    def products(i, row, block):
        cols = tile(block)
        act = nn(own[row, :ROWBLK, :feat], jnp.concatenate([gate_own[:, cols], up_own[:, cols]], axis=1))
        act += nn(other[row, :ROWBLK, :feat], jnp.concatenate([gate_other[:, cols], up_other[:, cols]], axis=1))
        grad = nt(own[row, :ROWBLK, feat:], down_own[cols, :]) + nt(other[row, :ROWBLK, feat:], down_other[cols, :])
        out[tile(i), : 2 * BLK] = act.astype(out.dtype)
        out[tile(i), 2 * BLK :] = grad.astype(out.dtype)

    def some_base(n, c):
        for j in range(2 * BASE):
            i = n * 2 * BASE + j
            products(i, core * (t.rows // 2) + n * 2 + j // BASE, table[t.base + core * base + i])
        return c

    def some_extra(n, c):
        for j in range(2):
            i = n * 2 + j
            k = core * extra + i
            products(base + i, table[t.unit_row + k // EXTRA], table[t.extra + k])
        return c

    lax.fori_loop(0, base // (2 * BASE), some_base, 0)
    lax.fori_loop(0, extra // 2, some_extra, 0, unroll=extra // 2 if units <= 3 else 1)


def listed(t, units, at):
    base, extra = BASE * t.rows // 2, EXTRA * units // 2
    e = at - 2 * base
    in_base = at + jnp.where(at >= base, extra, 0)
    return jnp.where(e < 0, in_base, base + e + jnp.where(e >= extra, base, 0))


def load_acts(t, units, place, blocks, acts, sems):
    quarter = (BASE * t.rows + EXTRA * units) * BLK // 8
    core, x, zh = place[0], place[1], place[2]
    piece = quarter // 4
    waits = []
    for k, whose in enumerate((core, 1 - core)):
        own, near, far = blocks[3 * k : 3 * k + 3]
        for ref, skip, d in ((own, 0, 0), (near, 0, 3), (near, quarter, 1), (far, 0, 2)):
            first, sem = pl.multiple_of((4 * whose + (x + d) % 4) * quarter, 16), sems.at[len(waits)]

            def start(p, c, ref=ref, skip=skip, first=first, sem=sem):
                source = ref.at[pl.ds(pl.multiple_of(skip + p * piece, 16), piece)]
                to = pl.multiple_of(first + (zh + p) % 4 * piece, 16)
                pltpu.make_async_copy(source, acts.at[pl.ds(to, piece)], sem).start()
                return c

            lax.fori_loop(0, 4, start, 0)
            waits.append(pltpu.make_async_copy(ref.at[pl.ds(skip, quarter)], acts.at[pl.ds(first, quarter)], sem))
    for wait in waits:
        wait.wait()


def rows_kernel(t, units, place, table, *refs):
    halves, (gate, up, down, out, acts, total, done, sems) = refs[:6], refs[6:]
    feat = down.shape[1]
    load_acts(t, units, place, halves, acts, sems)

    def products(at, picks):
        fwd, bwd = 0.0, 0.0
        for j, b in enumerate(picks):
            act, cols = acts[tile(listed(t, units, at + j)), :], tile(b)
            fwd += nn(act[:, :BLK], down[cols, :])
            bwd += nt(act[:, BLK:], jnp.concatenate([gate[:, cols], up[:, cols]], axis=1))
        return fwd, bwd

    def row(r, c):
        fwd, bwd = products(BASE * r, [table[t.base + BASE * r + j] for j in range(BASE)])
        total[:, :feat] = fwd
        total[:, feat:] = bwd
        u = table[t.row_unit + r]

        @pl.when(u >= 0)
        def _():
            fwd, bwd = products(BASE * t.rows + EXTRA * u, [table[t.extra + EXTRA * u + j] for j in range(EXTRA)])
            total[:, :feat] += fwd
            total[:, feat:] += bwd

        done[tile(r), :] = total[...].astype(done.dtype)
        pltpu.make_async_copy(done.at[tile(r)], out.at[tile(r)], sems.at[8]).start()
        return c

    lax.fori_loop(0, t.rows, row, 0)
    pltpu.make_async_copy(done, out, sems.at[8]).wait()


def weights_kernel(t, units, together, scale, place, table, *refs):
    halves, (rows, grad_gate, grad_up, grad_down, acts, turned, sems) = refs[:6], refs[6:]
    feat = grad_down.shape[1]
    step = pl.program_id(0)

    @pl.when(step == 0)
    def _():
        load_acts(t, units, place, halves, acts, sems)
        acts[tile(t.pairs), :] = jnp.zeros((BLK, acts.shape[1]), acts.dtype)

        def turn(r, c):
            turned[:, tile(r)] = rows[r, :ROWBLK, :feat].T
            return c

        lax.fori_loop(0, t.rows, turn, 0)

    for ref in (grad_gate, grad_up, grad_down):
        ref[...] = jnp.zeros_like(ref)

    def block(i, c):
        b = step * together + i

        def two(j, c):
            live = t.rows * b + 2 * j
            picked = [table[t.live_row + live], table[t.live_row + live + 1]]
            act = jnp.concatenate([acts[tile(listed(t, units, table[t.live_at + live + k])), :] for k in (0, 1)], axis=0)
            both = nn(jnp.concatenate([turned[:, tile(r)] for r in picked], axis=1), act[:, BLK:]) * scale
            cot = jnp.concatenate([rows[r, :ROWBLK, feat:] for r in picked], axis=0)
            grad_gate[:, tile(i)] += both[:, :BLK]
            grad_up[:, tile(i)] += both[:, BLK:]
            grad_down[tile(i), :] += nn(act[:, :BLK].T, cot) * scale
            return c

        return lax.fori_loop(0, (table[t.live + b] + 1) // 2, two, c)

    lax.fori_loop(0, together, block, 0)


def copies(array, axis):
    n = lax.axis_size(axis)
    return lax.all_to_all(jnp.broadcast_to(array[None], (n, *array.shape)), axis, 0, 0, tiled=True)


def across(array):
    return lax.ppermute(array, "core", [(0, 1), (1, 0)])


def ring(array, axis):
    def onward(array, d):
        return lax.ppermute(array, axis, [(i, (i + d) % 4) for i in range(4)])

    half = array.shape[0] // 2
    before, after = onward(array, 1), onward(array, -1)
    return before, after, jnp.concatenate([onward(before[:half], 1), onward(after[half:], -1)], axis=0)


def summed(array, axis):
    n = lax.axis_size(axis)
    tiles = array.reshape(n, array.shape[0] // n, array.shape[1])
    return lax.all_to_all(tiles, axis, 0, 0, tiled=True).astype(F32).sum(axis=0)


def summed_scaled(array, axis):
    n = lax.axis_size(axis)
    size, columns = array.shape[0] // n, array.shape[1]
    peak = jnp.max(jnp.abs(array), axis=0, keepdims=True)
    power = jnp.round(jnp.clip(jnp.log2(jnp.maximum(peak, 1e-36)), -119.0, 119.0))
    tiles = (array * jnp.exp2(-power)).astype(jnp.float16).reshape(n, size, columns)
    powers = jnp.broadcast_to(power.astype(jnp.float16), (n, 16, columns))
    arrived = lax.all_to_all(jnp.concatenate([tiles, powers], axis=1), axis, 0, 0, tiled=True).astype(F32)
    return jnp.sum(arrived[:, :size] * jnp.exp2(arrived[:, size : size + 1]), axis=0)


def activations(parts, by_ring):
    sums = summed_scaled(summed(parts, "x"), "zh")
    gate, up, grad = sums[:, :BLK], sums[:, BLK : 2 * BLK], sums[:, 2 * BLK :]
    s = jax.nn.sigmoid(gate)
    acts = jnp.concatenate(
        [
            (jax.nn.silu(gate) * up).astype(BF16),
            (grad * up * s * (1.0 + gate * (1.0 - s))).astype(BF16),
            (grad * gate * s).astype(BF16),
        ],
        axis=1,
    )
    if by_ring:
        before, after, far = ring(acts, "zh")
        own = jnp.concatenate([acts, after, far, before], axis=0)
        before, after, far = ring(own, "x")
        near = jnp.concatenate([before, after], axis=0)
        return own, near, far, across(own), across(near), across(far)
    acts = copies(copies(acts, "zh").reshape(-1, 3 * BLK), "x")
    halves = []
    for half in (acts, across(acts)):
        halves += [half[0], jnp.concatenate([half[3], half[1]], axis=0), half[2]]
    return halves


def from_rows(units, place, table, rows, rows_other, gate, gate_other, up, up_other, down, down_other, t):
    feat = down.shape[1]
    parts = pl.pallas_call(
        functools.partial(partials_kernel, t, units, feat),
        out_shape=jax.ShapeDtypeStruct(((BASE * t.rows + EXTRA * units) // 2 * ROWBLK, 3 * BLK), BF16),
        in_specs=[SMEM, SMEM] + [VMEM] * 8,
        out_specs=VMEM,
        compiler_params=PARAMS,
        name="partials",
    )(place, table, rows, rows_other, gate, gate_other, up, up_other, down, down_other)
    by_ring = units < t.rows
    acts = activations(parts, by_ring)
    if not by_ring:
        place = jnp.concatenate([place[:1], jnp.zeros_like(place[1:])])

    scratch = [pltpu.VMEM(((t.pairs + 1) * BLK, 3 * BLK), BF16)]
    partial_rows = pl.pallas_call(
        functools.partial(rows_kernel, t, units),
        out_shape=jax.ShapeDtypeStruct((t.rows * ROWBLK, 2 * feat), BF16),
        in_specs=[SMEM, SMEM] + [ANY] * 6 + [VMEM] * 3,
        out_specs=pl.BlockSpec(memory_space=pltpu.HBM),
        scratch_shapes=scratch
        + [
            pltpu.VMEM((ROWBLK, 2 * feat), F32),
            pltpu.VMEM((t.rows * ROWBLK, 2 * feat), BF16),
            pltpu.SemaphoreType.DMA((9,)),
        ],
        compiler_params=PARAMS,
        name="row_grads",
    )(place, table, *acts, gate, up, down)
    out_rows = summed(partial_rows, TP).astype(BF16)

    together = 2 if t.blocks % 2 == 0 else 1
    columns = pl.BlockSpec((feat, together * BLK), lambda b: (0, b))
    grad_gate, grad_up, grad_down = pl.pallas_call(
        functools.partial(weights_kernel, t, units, together, (t.rows * ROWBLK) ** -0.5),
        grid=(t.blocks // together,),
        out_shape=(
            jax.ShapeDtypeStruct(gate.shape, F32),
            jax.ShapeDtypeStruct(up.shape, F32),
            jax.ShapeDtypeStruct(down.shape, F32),
        ),
        in_specs=[SMEM, SMEM] + [ANY] * 6 + [VMEM],
        out_specs=(columns, columns, pl.BlockSpec((together * BLK, feat), lambda b: (b, 0))),
        scratch_shapes=scratch + [pltpu.VMEM((feat, t.rows * ROWBLK), BF16), pltpu.SemaphoreType.DMA((8,))],
        compiler_params=PARAMS,
        name="weight_grads",
    )(place, table, *acts, rows)
    return out_rows[:, :feat], out_rows[:, feat:], grad_gate, grad_up, grad_down


def shards(tokens, gate, up, down, masks, cotangent):
    own_rows, feat = tokens.shape
    t = Table(*masks.shape)
    place = jnp.stack([lax.axis_index(axis) for axis in ("core", "x", "zh")]).astype(jnp.int32)
    payload = pl.pallas_call(
        functools.partial(payload_kernel, BASE),
        out_shape=jax.ShapeDtypeStruct((lax.axis_size(TP), own_rows + 16, 2 * feat), BF16),
        in_specs=[SMEM, VMEM, VMEM],
        out_specs=VMEM,
        name="payload",
    )(masks, tokens, cotangent)
    table = pl.pallas_call(
        functools.partial(table_kernel, t),
        out_shape=jax.ShapeDtypeStruct((t.size,), jnp.int32),
        in_specs=[SMEM],
        out_specs=SMEM,
        name="pair_table",
    )(masks)
    gate_other, up_other, down_other = across(gate), across(up), across(down)
    rows = lax.all_to_all(payload, TP, 0, 0, tiled=True)
    rows, table, gate_other, up_other, down_other = lax.optimization_barrier(
        (rows, table, gate_other, up_other, down_other)
    )
    rows_other = across(rows)
    most = jnp.max(rows[:, own_rows, 0].astype(F32))
    path = sum((most > room).astype(jnp.int32) for room in ROOM[:-1])
    paths = [functools.partial(from_rows, units, t=t) for units in ROOM]
    return lax.switch(
        path, paths, place, table, rows, rows_other, gate, gate_other, up, up_other, down, down_other
    )


def solution(mesh):
    fine = Mesh(mesh.devices.reshape(4, 4, 2, 2, 4), SEQ + TP)
    wide, tall = P(SEQ, TP), P(TP, SEQ)
    return jax.shard_map(
        shards,
        mesh=fine,
        in_specs=(tall, wide, wide, tall, P(None, TP), tall),
        out_specs=(tall, tall, wide, wide, tall),
        check_vma=False,
    )
```

```python
import functools

import jax
import jax.numpy as jnp
from jax import lax
from jax.experimental import pallas as pl
from jax.experimental.pallas import tpu as pltpu
from jax.sharding import Mesh, PartitionSpec as P

BLK = 128
ROWBLK = 128
BASE = 3
EXTRA = 4
ROOM = (2, 3, 8)
SEQ = ("x", "zh", "core")
TP = ("zl", "y")
BF16 = jnp.bfloat16
F32 = jnp.float32
ANY = pl.BlockSpec(memory_space=pl.ANY)
VMEM = pl.BlockSpec(memory_space=pltpu.VMEM)
SMEM = pl.BlockSpec(memory_space=pltpu.SMEM)
PARAMS = pltpu.CompilerParams(vmem_limit_bytes=40 << 20)


def nt(a, b):
    return lax.dot_general(a, b, (((1,), (1,)), ((), ())), preferred_element_type=F32)


def nn(a, b):
    return jnp.dot(a, b, preferred_element_type=F32)


def tile(i):
    if isinstance(i, int):
        return pl.ds(i * BLK, BLK)
    return pl.ds(pl.multiple_of(i * BLK, BLK), BLK)


class Table:
    def __init__(self, rows, blocks):
        self.rows, self.blocks = rows, blocks
        self.base = 0
        self.extra = self.base + BASE * rows
        self.unit_row = self.extra + EXTRA * rows
        self.row_unit = self.unit_row + rows
        self.live_row = self.row_unit + rows
        self.live_at = self.live_row + rows * blocks
        self.live = self.live_at + rows * blocks
        self.spare = self.live + blocks
        self.size = self.spare + 1
        self.pairs = (BASE + EXTRA) * rows


def payload_kernel(blocks_kept, masks, tokens, cotangent, out):
    rows, feat = tokens.shape
    heavy = jnp.int32(0)
    for r in range(masks.shape[0]):
        kept = sum(masks[r, b] for b in range(masks.shape[1]))
        heavy += (kept > blocks_kept).astype(jnp.int32)
    count = jnp.full((out.shape[1] - rows, out.shape[2]), heavy.astype(F32)).astype(out.dtype)
    for k in range(out.shape[0]):
        out[k, :rows, :feat] = tokens[...]
        out[k, :rows, feat:] = cotangent[...]
        out[k, rows:, :] = count


def table_kernel(t, masks, out):
    for k in range(t.extra, t.row_unit):
        out[k] = 0
    for k in range(t.rows * t.blocks):
        out[t.live_row + k] = 0
        out[t.live_at + k] = t.pairs

    def row(r, c):
        units, live = c[0], list(c[1:])
        count = jnp.int32(0)
        for b in range(t.blocks):
            one = masks[r, b]
            kept, based = one == 1, count < BASE
            at = jnp.where(based, BASE * r, BASE * (t.rows - 1) + EXTRA * units) + count
            out[jnp.where(kept, t.base + at, t.spare)] = b
            out[jnp.where(kept, t.live_row + t.rows * b + live[b], t.spare)] = r
            out[jnp.where(kept, t.live_at + t.rows * b + live[b], t.spare)] = at
            live[b] += one
            count += one
        heavy = count > BASE
        out[t.row_unit + r] = jnp.where(heavy, units, -1)
        out[jnp.where(heavy, t.unit_row + units, t.spare)] = r
        return units + heavy.astype(jnp.int32), *live

    _, *live = lax.fori_loop(0, t.rows, row, (jnp.int32(0),) * (t.blocks + 1))
    for b in range(t.blocks):
        out[t.live + b] = live[b]


def partials_kernel(t, units, feat, place, table, own, other, gate_own, gate_other, up_own, up_other, down_own,
                    down_other, out):
    core = place[0]
    base, extra = BASE * t.rows // 2, EXTRA * units // 2

    def products(i, row, block):
        cols = tile(block)
        act = nn(own[row, :ROWBLK, :feat], jnp.concatenate([gate_own[:, cols], up_own[:, cols]], axis=1))
        act += nn(other[row, :ROWBLK, :feat], jnp.concatenate([gate_other[:, cols], up_other[:, cols]], axis=1))
        grad = nt(own[row, :ROWBLK, feat:], down_own[cols, :]) + nt(other[row, :ROWBLK, feat:], down_other[cols, :])
        out[tile(i), : 2 * BLK] = act.astype(out.dtype)
        out[tile(i), 2 * BLK :] = grad.astype(out.dtype)

    def some_base(n, c):
        for j in range(2 * BASE):
            i = n * 2 * BASE + j
            products(i, core * (t.rows // 2) + n * 2 + j // BASE, table[t.base + core * base + i])
        return c

    def some_extra(n, c):
        for j in range(2):
            i = n * 2 + j
            k = core * extra + i
            products(base + i, table[t.unit_row + k // EXTRA], table[t.extra + k])
        return c

    narrow = units < t.rows
    lax.fori_loop(0, base // (2 * BASE), some_base, 0, unroll=narrow)
    lax.fori_loop(0, extra // 2, some_extra, 0, unroll=narrow)


def listed(t, units, at):
    base, extra = BASE * t.rows // 2, EXTRA * units // 2
    e = at - 2 * base
    in_base = at + jnp.where(at >= base, extra, 0)
    return jnp.where(e < 0, in_base, base + e + jnp.where(e >= extra, base, 0))


def load_acts(t, units, place, blocks, acts, sems):
    quarter = (BASE * t.rows + EXTRA * units) * BLK // 8
    core, x = place[0], place[1]
    moves = []
    for k, whose in enumerate((core, 1 - core)):
        own, near, far = blocks[3 * k : 3 * k + 3]
        for ref, skip, d in ((own, 0, 0), (near, 0, 3), (near, quarter, 1), (far, 0, 2)):
            start = pl.multiple_of((4 * whose + (x + d) % 4) * quarter, 16)
            source, target = ref.at[pl.ds(skip, quarter)], acts.at[pl.ds(start, quarter)]
            moves.append(pltpu.make_async_copy(source, target, sems.at[len(moves)]))
    for move in moves:
        move.start()
    for move in moves:
        move.wait()


def rows_kernel(t, units, place, table, *refs):
    halves, (gate, up, down, out, acts, total, done, sems) = refs[:6], refs[6:]
    feat = down.shape[1]
    load_acts(t, units, place, halves, acts, sems)

    def products(at, picks):
        fwd, bwd = 0.0, 0.0
        for j, b in enumerate(picks):
            act, cols = acts[tile(listed(t, units, at + j)), :], tile(b)
            fwd += nn(act[:, :BLK], down[cols, :])
            bwd += nt(act[:, BLK:], jnp.concatenate([gate[:, cols], up[:, cols]], axis=1))
        return fwd, bwd

    def row(r, c):
        fwd, bwd = products(BASE * r, [table[t.base + BASE * r + j] for j in range(BASE)])
        total[:, :feat] = fwd
        total[:, feat:] = bwd
        u = table[t.row_unit + r]

        @pl.when(u >= 0)
        def _():
            fwd, bwd = products(BASE * t.rows + EXTRA * u, [table[t.extra + EXTRA * u + j] for j in range(EXTRA)])
            total[:, :feat] += fwd
            total[:, feat:] += bwd

        done[tile(r), :] = total[...].astype(done.dtype)
        pltpu.make_async_copy(done.at[tile(r)], out.at[tile(r)], sems.at[8]).start()
        return c

    lax.fori_loop(0, t.rows, row, 0, unroll=2 if units < t.rows else 1)
    pltpu.make_async_copy(done, out, sems.at[8]).wait()


def weights_kernel(t, units, together, scale, place, table, *refs):
    halves, (rows, grad_gate, grad_up, grad_down, acts, turned, sems) = refs[:6], refs[6:]
    feat = grad_down.shape[1]
    step = pl.program_id(0)

    @pl.when(step == 0)
    def _():
        load_acts(t, units, place, halves, acts, sems)
        acts[tile(t.pairs), :] = jnp.zeros((BLK, acts.shape[1]), acts.dtype)

        def turn(r, c):
            turned[:, tile(r)] = rows[r, :ROWBLK, :feat].T
            return c

        lax.fori_loop(0, t.rows, turn, 0)

    for ref in (grad_gate, grad_up, grad_down):
        ref[...] = jnp.zeros_like(ref)

    def block(i, c):
        b = step * together + i

        def two(j, c):
            live = t.rows * b + 2 * j
            picked = [table[t.live_row + live], table[t.live_row + live + 1]]
            act = jnp.concatenate([acts[tile(listed(t, units, table[t.live_at + live + k])), :] for k in (0, 1)], axis=0)
            both = nn(jnp.concatenate([turned[:, tile(r)] for r in picked], axis=1), act[:, BLK:]) * scale
            cot = jnp.concatenate([rows[r, :ROWBLK, feat:] for r in picked], axis=0)
            grad_gate[:, tile(i)] += both[:, :BLK]
            grad_up[:, tile(i)] += both[:, BLK:]
            grad_down[tile(i), :] += nn(act[:, :BLK].T, cot) * scale
            return c

        return lax.fori_loop(0, (table[t.live + b] + 1) // 2, two, c)

    lax.fori_loop(0, together, block, 0)


def copies(array, axis):
    n = lax.axis_size(axis)
    return lax.all_to_all(jnp.broadcast_to(array[None], (n, *array.shape)), axis, 0, 0, tiled=True)


def across(array):
    return lax.ppermute(array, "core", [(0, 1), (1, 0)])


def onward(array, d):
    n = lax.axis_size("x")
    return lax.ppermute(array, "x", [(i, (i + d) % n) for i in range(n)])


def summed(array, axis):
    n = lax.axis_size(axis)
    tiles = array.reshape(n, array.shape[0] // n, array.shape[1])
    return lax.all_to_all(tiles, axis, 0, 0, tiled=True).astype(F32).sum(axis=0)


def summed_scaled(array, axis):
    n = lax.axis_size(axis)
    size, columns = array.shape[0] // n, array.shape[1]
    peak = jnp.max(jnp.abs(array), axis=0, keepdims=True)
    power = jnp.round(jnp.clip(jnp.log2(jnp.maximum(peak, 1e-36)), -119.0, 119.0))
    tiles = (array * jnp.exp2(-power)).astype(jnp.float16).reshape(n, size, columns)
    powers = jnp.broadcast_to(power.astype(jnp.float16), (n, 16, columns))
    arrived = lax.all_to_all(jnp.concatenate([tiles, powers], axis=1), axis, 0, 0, tiled=True).astype(F32)
    return jnp.sum(arrived[:, :size] * jnp.exp2(arrived[:, size : size + 1]), axis=0)


def activations(parts):
    sums = summed_scaled(summed(parts, "x"), "zh")
    gate, up, grad = sums[:, :BLK], sums[:, BLK : 2 * BLK], sums[:, 2 * BLK :]
    s = jax.nn.sigmoid(gate)
    acts = jnp.concatenate(
        [
            (jax.nn.silu(gate) * up).astype(BF16),
            (grad * up * s * (1.0 + gate * (1.0 - s))).astype(BF16),
            (grad * gate * s).astype(BF16),
        ],
        axis=1,
    )
    own = copies(acts, "zh").reshape(-1, 3 * BLK)
    half = own.shape[0] // 2
    before, after = onward(own, 1), onward(own, -1)
    far = jnp.concatenate([onward(before[:half], 1), onward(after[half:], -1)], axis=0)
    blocks = own, jnp.concatenate([before, after], axis=0), far
    return *blocks, *map(across, blocks)


def from_rows(units, place, table, rows, rows_other, gate, gate_other, up, up_other, down, down_other, t):
    feat = down.shape[1]
    parts = pl.pallas_call(
        functools.partial(partials_kernel, t, units, feat),
        out_shape=jax.ShapeDtypeStruct(((BASE * t.rows + EXTRA * units) // 2 * ROWBLK, 3 * BLK), BF16),
        in_specs=[SMEM, SMEM] + [VMEM] * 8,
        out_specs=VMEM,
        compiler_params=PARAMS,
        name="partials",
    )(place, table, rows, rows_other, gate, gate_other, up, up_other, down, down_other)
    acts = activations(parts)

    scratch = [pltpu.VMEM(((t.pairs + 1) * BLK, 3 * BLK), BF16)]
    partial_rows = pl.pallas_call(
        functools.partial(rows_kernel, t, units),
        out_shape=jax.ShapeDtypeStruct((t.rows * ROWBLK, 2 * feat), BF16),
        in_specs=[SMEM, SMEM] + [ANY] * 6 + [VMEM] * 3,
        out_specs=pl.BlockSpec(memory_space=pltpu.HBM),
        scratch_shapes=scratch
        + [
            pltpu.VMEM((ROWBLK, 2 * feat), F32),
            pltpu.VMEM((t.rows * ROWBLK, 2 * feat), BF16),
            pltpu.SemaphoreType.DMA((9,)),
        ],
        compiler_params=PARAMS,
        name="row_grads",
    )(place, table, *acts, gate, up, down)
    out_rows = summed(partial_rows, TP).astype(BF16)

    together = 2 if t.blocks % 2 == 0 else 1
    columns = pl.BlockSpec((feat, together * BLK), lambda b: (0, b))
    grad_gate, grad_up, grad_down = pl.pallas_call(
        functools.partial(weights_kernel, t, units, together, (t.rows * ROWBLK) ** -0.5),
        grid=(t.blocks // together,),
        out_shape=(
            jax.ShapeDtypeStruct(gate.shape, F32),
            jax.ShapeDtypeStruct(up.shape, F32),
            jax.ShapeDtypeStruct(down.shape, F32),
        ),
        in_specs=[SMEM, SMEM] + [ANY] * 6 + [VMEM],
        out_specs=(columns, columns, pl.BlockSpec((together * BLK, feat), lambda b: (b, 0))),
        scratch_shapes=scratch + [pltpu.VMEM((feat, t.rows * ROWBLK), BF16), pltpu.SemaphoreType.DMA((8,))],
        compiler_params=PARAMS,
        name="weight_grads",
    )(place, table, *acts, rows)
    return out_rows[:, :feat], out_rows[:, feat:], grad_gate, grad_up, grad_down


def shards(tokens, gate, up, down, masks, cotangent):
    own_rows, feat = tokens.shape
    t = Table(*masks.shape)
    place = jnp.stack([lax.axis_index("core"), lax.axis_index("x")]).astype(jnp.int32)
    payload = pl.pallas_call(
        functools.partial(payload_kernel, BASE),
        out_shape=jax.ShapeDtypeStruct((lax.axis_size(TP), own_rows + 16, 2 * feat), BF16),
        in_specs=[SMEM, VMEM, VMEM],
        out_specs=VMEM,
        name="payload",
    )(masks, tokens, cotangent)
    table = pl.pallas_call(
        functools.partial(table_kernel, t),
        out_shape=jax.ShapeDtypeStruct((t.size,), jnp.int32),
        in_specs=[SMEM],
        out_specs=SMEM,
        name="pair_table",
    )(masks)
    gate_other, up_other, down_other = across(gate), across(up), across(down)
    rows = lax.all_to_all(payload, TP, 0, 0, tiled=True)
    rows, table, gate_other, up_other, down_other = lax.optimization_barrier(
        (rows, table, gate_other, up_other, down_other)
    )
    rows_other = across(rows)
    most = jnp.max(rows[:, own_rows, 0].astype(F32))
    path = sum((most > room).astype(jnp.int32) for room in ROOM[:-1])
    paths = [functools.partial(from_rows, units, t=t) for units in ROOM]
    return lax.switch(
        path, paths, place, table, rows, rows_other, gate, gate_other, up, up_other, down, down_other
    )


def solution(mesh):
    fine = Mesh(mesh.devices.reshape(4, 4, 2, 2, 4), SEQ + TP)
    wide, tall = P(SEQ, TP), P(TP, SEQ)
    return jax.shard_map(
        shards,
        mesh=fine,
        in_specs=(tall, wide, wide, tall, P(None, TP), tall),
        out_specs=(tall, tall, wide, wide, tall),
        check_vma=False,
    )
```

```python
import functools

import jax
import jax.numpy as jnp
from jax import lax
from jax.experimental import pallas as pl
from jax.experimental.pallas import tpu as pltpu
from jax.sharding import Mesh, PartitionSpec as P

BLK = 128
ROWBLK = 128
BASE = 3
EXTRA = 4
ROOM = (2, 3, 8)
SEQ = ("x", "zh", "core")
TP = ("zl", "y")
BF16 = jnp.bfloat16
F32 = jnp.float32
ANY = pl.BlockSpec(memory_space=pl.ANY)
VMEM = pl.BlockSpec(memory_space=pltpu.VMEM)
SMEM = pl.BlockSpec(memory_space=pltpu.SMEM)
PARAMS = pltpu.CompilerParams(vmem_limit_bytes=40 << 20)


def nt(a, b):
    return lax.dot_general(a, b, (((1,), (1,)), ((), ())), preferred_element_type=F32)


def nn(a, b):
    return jnp.dot(a, b, preferred_element_type=F32)


def tile(i):
    if isinstance(i, int):
        return pl.ds(i * BLK, BLK)
    return pl.ds(pl.multiple_of(i * BLK, BLK), BLK)


class Table:
    def __init__(self, rows, blocks):
        self.rows, self.blocks = rows, blocks
        self.base = 0
        self.extra = self.base + BASE * rows
        self.unit_row = self.extra + EXTRA * rows
        self.row_unit = self.unit_row + rows
        self.live_row = self.row_unit + rows
        self.live_at = self.live_row + rows * blocks
        self.live = self.live_at + rows * blocks
        self.spare = self.live + blocks
        self.size = self.spare + 1
        self.pairs = (BASE + EXTRA) * rows


def payload_kernel(blocks_kept, masks, tokens, cotangent, out):
    rows, feat = tokens.shape
    heavy = jnp.int32(0)
    for r in range(masks.shape[0]):
        kept = sum(masks[r, b] for b in range(masks.shape[1]))
        heavy += (kept > blocks_kept).astype(jnp.int32)
    count = jnp.full((out.shape[1] - rows, out.shape[2]), heavy.astype(F32)).astype(out.dtype)
    for k in range(out.shape[0]):
        out[k, :rows, :feat] = tokens[...]
        out[k, :rows, feat:] = cotangent[...]
        out[k, rows:, :] = count


def table_kernel(t, masks, out):
    for k in range(t.extra, t.row_unit):
        out[k] = 0
    for k in range(t.rows * t.blocks):
        out[t.live_row + k] = 0
        out[t.live_at + k] = t.pairs

    def row(r, c):
        units, live = c[0], list(c[1:])
        count = jnp.int32(0)
        for b in range(t.blocks):
            one = masks[r, b]
            kept, based = one == 1, count < BASE
            at = jnp.where(based, BASE * r, BASE * (t.rows - 1) + EXTRA * units) + count
            out[jnp.where(kept, t.base + at, t.spare)] = b
            out[jnp.where(kept, t.live_row + t.rows * b + live[b], t.spare)] = r
            out[jnp.where(kept, t.live_at + t.rows * b + live[b], t.spare)] = at
            live[b] += one
            count += one
        heavy = count > BASE
        out[t.row_unit + r] = jnp.where(heavy, units, -1)
        out[jnp.where(heavy, t.unit_row + units, t.spare)] = r
        return units + heavy.astype(jnp.int32), *live

    _, *live = lax.fori_loop(0, t.rows, row, (jnp.int32(0),) * (t.blocks + 1))
    for b in range(t.blocks):
        out[t.live + b] = live[b]


def partials_kernel(t, units, feat, place, table, own, other, gate_own, gate_other, up_own, up_other, down_own,
                    down_other, out):
    core = place[0]
    base, extra = BASE * t.rows // 2, EXTRA * units // 2

    def products(i, row, block):
        cols = tile(block)
        act = nn(own[row, :ROWBLK, :feat], jnp.concatenate([gate_own[:, cols], up_own[:, cols]], axis=1))
        act += nn(other[row, :ROWBLK, :feat], jnp.concatenate([gate_other[:, cols], up_other[:, cols]], axis=1))
        grad = nt(own[row, :ROWBLK, feat:], down_own[cols, :]) + nt(other[row, :ROWBLK, feat:], down_other[cols, :])
        out[tile(i), : 2 * BLK] = act.astype(out.dtype)
        out[tile(i), 2 * BLK :] = grad.astype(out.dtype)

    def some_base(n, c):
        for j in range(2 * BASE):
            i = n * 2 * BASE + j
            products(i, core * (t.rows // 2) + n * 2 + j // BASE, table[t.base + core * base + i])
        return c

    def some_extra(n, c):
        for j in range(2):
            i = n * 2 + j
            k = core * extra + i
            products(base + i, table[t.unit_row + k // EXTRA], table[t.extra + k])
        return c

    narrow = units < t.rows
    lax.fori_loop(0, base // (2 * BASE), some_base, 0, unroll=narrow)
    lax.fori_loop(0, extra // 2, some_extra, 0, unroll=narrow)


def listed(t, units, at):
    base, extra = BASE * t.rows // 2, EXTRA * units // 2
    e = at - 2 * base
    in_base = at + jnp.where(at >= base, extra, 0)
    return jnp.where(e < 0, in_base, base + e + jnp.where(e >= extra, base, 0))


def load_acts(t, units, place, blocks, acts, sems):
    quarter = (BASE * t.rows + EXTRA * units) * BLK // 8
    core, x = place[0], place[1]
    moves = []
    for k, whose in enumerate((core, 1 - core)):
        own, near, far = blocks[3 * k : 3 * k + 3]
        for ref, skip, d in ((own, 0, 0), (near, 0, 3), (near, quarter, 1), (far, 0, 2)):
            start = pl.multiple_of((4 * whose + (x + d) % 4) * quarter, 16)
            source, target = ref.at[pl.ds(skip, quarter)], acts.at[pl.ds(start, quarter)]
            moves.append(pltpu.make_async_copy(source, target, sems.at[len(moves)]))
    for move in moves:
        move.start()
    for move in moves:
        move.wait()


def rows_kernel(t, units, place, table, *refs):
    halves, (gate, up, down, out, acts, total, done, sems) = refs[:6], refs[6:]
    feat = down.shape[1]
    load_acts(t, units, place, halves, acts, sems)

    def products(at, picks):
        fwd, bwd = 0.0, 0.0
        for j, b in enumerate(picks):
            act, cols = acts[tile(listed(t, units, at + j)), :], tile(b)
            fwd += nn(act[:, :BLK], down[cols, :])
            bwd += nt(act[:, BLK:], jnp.concatenate([gate[:, cols], up[:, cols]], axis=1))
        return fwd, bwd

    def row(r, c):
        fwd, bwd = products(BASE * r, [table[t.base + BASE * r + j] for j in range(BASE)])
        total[:, :feat] = fwd
        total[:, feat:] = bwd
        u = table[t.row_unit + r]

        @pl.when(u >= 0)
        def _():
            fwd, bwd = products(BASE * t.rows + EXTRA * u, [table[t.extra + EXTRA * u + j] for j in range(EXTRA)])
            total[:, :feat] += fwd
            total[:, feat:] += bwd

        done[tile(r), :] = total[...].astype(done.dtype)
        pltpu.make_async_copy(done.at[tile(r)], out.at[tile(r)], sems.at[8]).start()
        return c

    lax.fori_loop(0, t.rows, row, 0)
    pltpu.make_async_copy(done, out, sems.at[8]).wait()


def weights_kernel(t, units, together, scale, place, table, *refs):
    halves, (rows, grad_gate, grad_up, grad_down, acts, turned, sems) = refs[:6], refs[6:]
    feat = grad_down.shape[1]
    step = pl.program_id(0)

    @pl.when(step == 0)
    def _():
        load_acts(t, units, place, halves, acts, sems)
        acts[tile(t.pairs), :] = jnp.zeros((BLK, acts.shape[1]), acts.dtype)

        def turn(r, c):
            turned[:, tile(r)] = rows[r, :ROWBLK, :feat].T
            return c

        lax.fori_loop(0, t.rows, turn, 0)

    for ref in (grad_gate, grad_up, grad_down):
        ref[...] = jnp.zeros_like(ref)

    def block(i, c):
        b = step * together + i

        def two(j, c):
            live = t.rows * b + 2 * j
            picked = [table[t.live_row + live], table[t.live_row + live + 1]]
            act = jnp.concatenate([acts[tile(listed(t, units, table[t.live_at + live + k])), :] for k in (0, 1)], axis=0)
            both = nn(jnp.concatenate([turned[:, tile(r)] for r in picked], axis=1), act[:, BLK:]) * scale
            cot = jnp.concatenate([rows[r, :ROWBLK, feat:] for r in picked], axis=0)
            grad_gate[:, tile(i)] += both[:, :BLK]
            grad_up[:, tile(i)] += both[:, BLK:]
            grad_down[tile(i), :] += nn(act[:, :BLK].T, cot) * scale
            return c

        return lax.fori_loop(0, (table[t.live + b] + 1) // 2, two, c)

    lax.fori_loop(0, together, block, 0)


def copies(array, axis):
    n = lax.axis_size(axis)
    return lax.all_to_all(jnp.broadcast_to(array[None], (n, *array.shape)), axis, 0, 0, tiled=True)


def across(array):
    return lax.ppermute(array, "core", [(0, 1), (1, 0)])


def onward(array, d):
    n = lax.axis_size("x")
    return lax.ppermute(array, "x", [(i, (i + d) % n) for i in range(n)])


def summed(array, axis):
    n = lax.axis_size(axis)
    tiles = array.reshape(n, array.shape[0] // n, array.shape[1])
    return lax.all_to_all(tiles, axis, 0, 0, tiled=True).astype(F32).sum(axis=0)


def summed_scaled(array, axis):
    n = lax.axis_size(axis)
    size, columns = array.shape[0] // n, array.shape[1]
    peak = jnp.max(jnp.abs(array), axis=0, keepdims=True)
    power = jnp.round(jnp.clip(jnp.log2(jnp.maximum(peak, 1e-36)), -119.0, 119.0))
    tiles = (array * jnp.exp2(-power)).astype(jnp.float16).reshape(n, size, columns)
    powers = jnp.broadcast_to(power.astype(jnp.float16), (n, 16, columns))
    arrived = lax.all_to_all(jnp.concatenate([tiles, powers], axis=1), axis, 0, 0, tiled=True).astype(F32)
    return jnp.sum(arrived[:, :size] * jnp.exp2(arrived[:, size : size + 1]), axis=0)


def activations(parts):
    sums = summed_scaled(summed(parts, "x"), "zh")
    gate, up, grad = sums[:, :BLK], sums[:, BLK : 2 * BLK], sums[:, 2 * BLK :]
    s = jax.nn.sigmoid(gate)
    acts = jnp.concatenate(
        [
            (jax.nn.silu(gate) * up).astype(BF16),
            (grad * up * s * (1.0 + gate * (1.0 - s))).astype(BF16),
            (grad * gate * s).astype(BF16),
        ],
        axis=1,
    )
    own = copies(acts, "zh").reshape(-1, 3 * BLK)
    half = own.shape[0] // 2
    before, after = onward(own, 1), onward(own, -1)
    far = jnp.concatenate([onward(before[:half], 1), onward(after[half:], -1)], axis=0)
    blocks = own, jnp.concatenate([before, after], axis=0), far
    return *blocks, *map(across, blocks)


def from_rows(units, place, table, rows, rows_other, gate, gate_other, up, up_other, down, down_other, t):
    feat = down.shape[1]
    parts = pl.pallas_call(
        functools.partial(partials_kernel, t, units, feat),
        out_shape=jax.ShapeDtypeStruct(((BASE * t.rows + EXTRA * units) // 2 * ROWBLK, 3 * BLK), BF16),
        in_specs=[SMEM, SMEM] + [VMEM] * 8,
        out_specs=VMEM,
        compiler_params=PARAMS,
        name="partials",
    )(place, table, rows, rows_other, gate, gate_other, up, up_other, down, down_other)
    acts = activations(parts)

    scratch = [pltpu.VMEM(((t.pairs + 1) * BLK, 3 * BLK), BF16)]
    partial_rows = pl.pallas_call(
        functools.partial(rows_kernel, t, units),
        out_shape=jax.ShapeDtypeStruct((t.rows * ROWBLK, 2 * feat), BF16),
        in_specs=[SMEM, SMEM] + [ANY] * 6 + [VMEM] * 3,
        out_specs=pl.BlockSpec(memory_space=pltpu.HBM),
        scratch_shapes=scratch
        + [
            pltpu.VMEM((ROWBLK, 2 * feat), F32),
            pltpu.VMEM((t.rows * ROWBLK, 2 * feat), BF16),
            pltpu.SemaphoreType.DMA((9,)),
        ],
        compiler_params=PARAMS,
        name="row_grads",
    )(place, table, *acts, gate, up, down)
    out_rows = summed(partial_rows, TP).astype(BF16)

    together = 2 if t.blocks % 2 == 0 else 1
    columns = pl.BlockSpec((feat, together * BLK), lambda b: (0, b))
    grad_gate, grad_up, grad_down = pl.pallas_call(
        functools.partial(weights_kernel, t, units, together, (t.rows * ROWBLK) ** -0.5),
        grid=(t.blocks // together,),
        out_shape=(
            jax.ShapeDtypeStruct(gate.shape, F32),
            jax.ShapeDtypeStruct(up.shape, F32),
            jax.ShapeDtypeStruct(down.shape, F32),
        ),
        in_specs=[SMEM, SMEM] + [ANY] * 6 + [VMEM],
        out_specs=(columns, columns, pl.BlockSpec((together * BLK, feat), lambda b: (b, 0))),
        scratch_shapes=scratch + [pltpu.VMEM((feat, t.rows * ROWBLK), BF16), pltpu.SemaphoreType.DMA((8,))],
        compiler_params=PARAMS,
        name="weight_grads",
    )(place, table, *acts, rows)
    return out_rows[:, :feat], out_rows[:, feat:], grad_gate, grad_up, grad_down


def shards(tokens, gate, up, down, masks, cotangent):
    own_rows, feat = tokens.shape
    t = Table(*masks.shape)
    place = jnp.stack([lax.axis_index("core"), lax.axis_index("x")]).astype(jnp.int32)
    payload = pl.pallas_call(
        functools.partial(payload_kernel, BASE),
        out_shape=jax.ShapeDtypeStruct((lax.axis_size(TP), own_rows + 16, 2 * feat), BF16),
        in_specs=[SMEM, VMEM, VMEM],
        out_specs=VMEM,
        name="payload",
    )(masks, tokens, cotangent)
    table = pl.pallas_call(
        functools.partial(table_kernel, t),
        out_shape=jax.ShapeDtypeStruct((t.size,), jnp.int32),
        in_specs=[SMEM],
        out_specs=SMEM,
        name="pair_table",
    )(masks)
    gate_other, up_other, down_other = across(gate), across(up), across(down)
    rows = lax.all_to_all(payload, TP, 0, 0, tiled=True)
    rows, table, gate_other, up_other, down_other = lax.optimization_barrier(
        (rows, table, gate_other, up_other, down_other)
    )
    rows_other = across(rows)
    most = jnp.max(rows[:, own_rows, 0].astype(F32))
    path = sum((most > room).astype(jnp.int32) for room in ROOM[:-1])
    paths = [functools.partial(from_rows, units, t=t) for units in ROOM]
    return lax.switch(
        path, paths, place, table, rows, rows_other, gate, gate_other, up, up_other, down, down_other
    )


def solution(mesh):
    fine = Mesh(mesh.devices.reshape(4, 4, 2, 2, 4), SEQ + TP)
    wide, tall = P(SEQ, TP), P(TP, SEQ)
    return jax.shard_map(
        shards,
        mesh=fine,
        in_specs=(tall, wide, wide, tall, P(None, TP), tall),
        out_specs=(tall, tall, wide, wide, tall),
        check_vma=False,
    )
```
